128 devices in a mesh: row: 8 (over y, core), col: 16 (over x, z).
Axes of the slice: x: 4, y: 4, z: 4, core: 2. Of those that a mesh axis runs over, the one named last changes fastest.
Arguments:
- parent_front: float32 [4, 8, 256, 2, 16, 256], P(None, 'row', None, None, 'col'), may hold values from -6 to 48, as said below
- child_tiles: bfloat16 [128, 64, 256, 256], P(('row', 'col')), may hold values from -6 to 6
- tile_target: int32 [128, 64, 2], replicated, may hold values from 0 to 31, as said below
Outputs:
- factored_front: float32 [4, 8, 256, 2, 16, 256], P(None, 'row', None, None, 'col')
The draws below stay inside these ranges and needn't reach their ends.
Inputs may be any that keep to these rules, and one draw needn't show every extreme that they name: The leading 6 * 256 rows and columns of parent_front form a symmetric matrix with diagonal entries in 32 to 48 and other entries of magnitude at most 30 / 1536. tile_target[d, s] is the parent tile (row, column) into which tile s of device d is added (device d is mesh row d // 16, column d % 16); rows are 6 or more. Parent tile (I, J) lives on mesh row I % 8, column J % 16. The 64 tiles of one device go to 64 different devices, and one device receives a tile from every device.
All inputs are finite; a program needn't handle non-finite values.
Results may differ from the reference program's by a relative error of at most 0.0003.
Values may be sent and summed in bfloat16 or wider, within the bound.
No kernel may reach another device: no remote copies, remote signals or barrier semaphores. Data moves between devices by JAX's collectives and lax.ppermute only.
A program may use at most 192 MiB of HBM per device.

```python
import jax
import jax.numpy as jnp
from jax import lax

TILE = 256
PANELS = 6
LROWS = 4
PTILES = 32
LCOLS = 2
FRONT = 8192
STORED = 64
N_ROW = 8
N_COL = 16
DEVICES = 128


def draw_parent_front(key, part):
    key_base, key_raw, key_diag = jax.random.split(jax.random.fold_in(key, 5), 3)
    shape = (LROWS, N_ROW, TILE, LCOLS, N_COL, TILE)
    base = jnp.clip(jax.random.normal(key_base, shape, jnp.float32), -6.0, 6.0)
    order = PANELS * TILE
    bound = 30.0 / order
    raw = jax.random.uniform(key_raw, (order, order), jnp.float32, -bound, bound)
    symmetric = 0.5 * (raw + raw.T)
    diag = jax.random.uniform(key_diag, (order,), jnp.float32, 32.0, 48.0)
    identity = jnp.eye(order, dtype=jnp.float32)
    leading = symmetric * (1.0 - identity) + identity * diag[None, :]
    for first in range(PANELS):
        for second in range(PANELS):
            block = leading[first * TILE:(first + 1) * TILE, second * TILE:(second + 1) * TILE]
            base = base.at[first // N_ROW, first % N_ROW, :, second // N_COL, second % N_COL, :].set(block)
    return base


def draw_tile_target(key, part):
    busiest = jax.random.randint(jax.random.fold_in(key, 11), (), 0, DEVICES)
    keys = jax.random.split(jax.random.fold_in(key, 12), DEVICES)

    def one_device(device_key):
        key_perm, key_shuffle, key_rows, key_cols = jax.random.split(device_key, 4)
        others = jax.random.permutation(key_perm, DEVICES - 1).astype(jnp.int32)
        others = others + (others >= busiest).astype(jnp.int32)
        owners = jnp.concatenate([busiest.reshape(1).astype(jnp.int32), others[:STORED - 1]])
        owners = jax.random.permutation(key_shuffle, owners)
        owner_row = owners // N_COL
        owner_col = owners % N_COL
        lowest = jnp.maximum((PANELS - owner_row + N_ROW - 1) // N_ROW, 0).astype(jnp.int32)
        local_row = jax.random.randint(key_rows, (STORED,), lowest, LROWS)
        local_col = jax.random.randint(key_cols, (STORED,), 0, LCOLS)
        rows = owner_row + N_ROW * local_row
        cols = owner_col + N_COL * local_col
        return jnp.stack([rows, cols], axis=1).astype(jnp.int32)
    return jax.vmap(one_device)(keys)


def levels(own_key, dims, shards, smallest, high):
    loudness, own = 1.0, jax.random.fold_in(own_key, 6)
    for dim, shards_of in shards:
        heights = jnp.exp(jax.random.uniform(jax.random.fold_in(own, dim), (shards_of,), jnp.float32, smallest / len(shards), high / len(shards)))
        loudness = loudness * jnp.repeat(heights, dims[dim] // shards_of).reshape([-1 if axis == dim else 1 for axis in range(len(dims))])
    return loudness


def noise(own_key, extent, deviation, limit, cuts=(), kind=jnp.bfloat16):
    gain = levels(own_key, extent, cuts, -0.22, 0.18) if cuts else 1.0
    drawn = jax.random.normal(own_key, extent, jnp.float32) * deviation * gain
    return jnp.minimum(jnp.maximum(drawn, -limit), limit).astype(kind)


def setup_inputs(seed: int = 0) -> dict:
    arg_keys = jax.random.split(jax.random.key(seed), 4)
    parent_front = draw_parent_front(jax.random.fold_in(arg_keys[3], 71), 0)
    child_tiles = noise(arg_keys[1], (DEVICES, STORED, TILE, TILE), 1.0, 6.0, ((0, 128),))
    tile_target = draw_tile_target(jax.random.fold_in(arg_keys[3], 71), 0)
    return {"parent_front": parent_front, "child_tiles": child_tiles, "tile_target": tile_target}


def reference(parent_front, child_tiles, tile_target):
    tiles = parent_front.reshape(PTILES, TILE, PTILES, TILE)
    rows = tile_target[:, :, 0].reshape(-1)
    cols = tile_target[:, :, 1].reshape(-1)
    addend = child_tiles.reshape(-1, TILE, TILE).astype(jnp.float32)
    tiles = tiles.at[rows, :, cols, :].add(addend)
    front = tiles.reshape(FRONT, FRONT)
    for step in range(PANELS):
        start = step * TILE
        end = start + TILE
        lower = jnp.linalg.cholesky(front[start:end, start:end])
        panel = front[end:, start:end]
        solved = jax.scipy.linalg.solve_triangular(lower, panel.T, lower=True).T
        trailing = front[end:, end:] - jnp.dot(solved, solved.T, precision=lax.Precision.HIGHEST)
        front = front.at[start:end, start:end].set(lower)
        front = front.at[end:, start:end].set(solved)
        front = front.at[start:end, end:].set(jnp.zeros((TILE, FRONT - end), jnp.float32))
        front = front.at[end:, end:].set(trailing)
    return front.reshape(LROWS, N_ROW, TILE, LCOLS, N_COL, TILE)
```

```python
import jax
import jax.numpy as jnp
from jax import lax
from jax.experimental import pallas as pl
from jax.experimental.pallas import tpu as pltpu
from jax.sharding import PartitionSpec as P

PANELS = 6
BOTH = ("row", "col")
F32 = jnp.float32
BF16 = jnp.bfloat16
HIGHEST = lax.Precision.HIGHEST


def dot_nt(a, b):
    return lax.dot_general(
        a, b, (((1,), (1,)), ((), ())), precision=HIGHEST, preferred_element_type=F32
    )


def dot_nn(a, b):
    return lax.dot_general(
        a, b, (((1,), (0,)), ((), ())), precision=HIGHEST, preferred_element_type=F32
    )


def leading_kernel(tile, panels, places, a_ref, l_ref, w_ref, s_ref, acc_ref):
    rows = lax.broadcasted_iota(jnp.int32, (tile, tile), 0)
    cols = lax.broadcasted_iota(jnp.int32, (tile, tile), 1)
    diag = rows == cols
    eye = jnp.where(diag, 1.0, 0.0).astype(F32)
    weight = jnp.where(rows > cols, 1.0, jnp.where(diag, 0.5, 0.0)).astype(F32)

    def at(index):
        return pl.ds(pl.multiple_of(index * tile, tile), tile)

    for (i, j), (down, across) in places.items():
        s_ref[i * tile : (i + 1) * tile, j * tile : (j + 1) * tile] = a_ref[
            down * tile : (down + 1) * tile, across * tile : (across + 1) * tile
        ]
    l_ref[...] = jnp.zeros_like(l_ref)
    w_ref[...] = jnp.zeros_like(w_ref)

    @pl.loop(0, panels)
    def _(k):
        here = at(k)
        block = s_ref[here, here]
        only = jnp.where(diag, block, 0.0)
        down = lax.rsqrt(jnp.sum(only, axis=1, keepdims=True))
        across = lax.rsqrt(jnp.sum(only, axis=0, keepdims=True))
        w_ref[here, here] = jnp.where(diag, down, 0.0)
        acc_ref[...] = block * down * across - eye

        def improve():
            w = w_ref[here, here]
            w_ref[here, here] = w - dot_nn(acc_ref[...] * weight, w)

        def unfinished(state):
            step, worst = state
            return (worst > 1e-5) & (step < 16)

        def refine(state):
            step, _ = state
            improve()
            w = w_ref[here, here]
            left = dot_nt(dot_nn(w, s_ref[here, here]), w) - eye
            acc_ref[...] = left
            return step + 1, jnp.max(jnp.abs(left))

        lax.while_loop(unfinished, refine, (jnp.int32(0), jnp.max(jnp.abs(acc_ref[...]))))
        improve()
        l_ref[here, here] = jnp.where(
            rows >= cols, dot_nt(s_ref[here, here], w_ref[here, here]), 0.0
        )

        @pl.loop(k + 1, panels)
        def _(i):
            l_ref[at(i), here] = dot_nt(s_ref[at(i), here], w_ref[here, here])

        @pl.loop(k + 1, panels)
        def _(i):
            @pl.loop(k + 1, i + 1)
            def _(j):
                s_ref[at(i), at(j)] -= dot_nt(l_ref[at(i), here], l_ref[at(j), here])

    @pl.loop(1, panels)
    def _(i):
        @pl.loop(0, i)
        def _(j):
            acc_ref[...] = jnp.zeros_like(acc_ref)

            @pl.loop(j, i)
            def _(m):
                acc_ref[...] += dot_nn(l_ref[at(i), at(m)], w_ref[at(m), at(j)])

            w_ref[at(i), at(j)] = -dot_nn(w_ref[at(i), at(i)], acc_ref[...])


def factor_leading(packed, places, tile, panels):
    order = tile * panels
    whole = pl.BlockSpec(memory_space=pltpu.VMEM)
    return pl.pallas_call(
        lambda *refs: leading_kernel(tile, panels, places, *refs),
        out_shape=[jax.ShapeDtypeStruct((order, order), F32)] * 2,
        in_specs=[whole],
        out_specs=[whole] * 2,
        scratch_shapes=[pltpu.VMEM((order, order), F32), pltpu.VMEM((tile, tile), F32)],
        compiler_params=pltpu.CompilerParams(vmem_limit_bytes=44 << 20),
        cost_estimate=pl.CostEstimate(
            flops=12 * order**3, bytes_accessed=12 * order**2, transcendentals=0
        ),
        name="leading",
    )(packed)


def child_sum_kernel(hot_ref, child_ref, out_ref):
    @pl.when(pl.program_id(0) == 0)
    def _():
        out_ref[...] = jnp.zeros_like(out_ref)

    sources, pieces, stored, tile = child_ref.shape
    for e in range(pieces):
        right = child_ref[:, e].reshape(sources * stored, tile)
        out_ref[e] += jnp.dot(hot_ref[...], right, preferred_element_type=F32)


def child_sum(hot, child):
    devices, pieces, stored, tile = child.shape
    tiles = hot.shape[0]
    block = 8
    return pl.pallas_call(
        child_sum_kernel,
        out_shape=jax.ShapeDtypeStruct((pieces, tiles, tile), F32),
        grid=(devices // block,),
        in_specs=[
            pl.BlockSpec((tiles, block * stored), lambda g: (0, g)),
            pl.BlockSpec((block, pieces, stored, tile), lambda g: (g, 0, 0, 0)),
        ],
        out_specs=pl.BlockSpec((pieces, tiles, tile), lambda g: (0, 0, 0)),
        compiler_params=pltpu.CompilerParams(vmem_limit_bytes=24 << 20),
        cost_estimate=pl.CostEstimate(
            flops=2 * tiles * child.size,
            bytes_accessed=2 * (hot.size + child.size) + 4 * pieces * tiles * tile,
            transcendentals=0,
        ),
        name="child_sum",
    )(hot, child)


def shards(parent_front, child_tiles, tile_target):
    lrows = parent_front.shape[0]
    tile = parent_front.shape[2]
    lcols = parent_front.shape[3]
    row_count = lax.axis_size("row")
    col_count = lax.axis_size("col")
    devices = row_count * col_count
    stride = col_count // row_count
    order = PANELS * tile
    part = tile // col_count
    deep = part // row_count
    slots = lrows * lcols
    my_row = lax.axis_index("row")
    my_col = lax.axis_index("col")
    front = parent_front.reshape(lrows, tile, lcols, tile)
    stored = child_tiles.shape[1]

    base = front[:, :, 0, :].reshape(lrows, col_count, part, tile).transpose(1, 0, 2, 3)
    base = lax.all_to_all(base, "col", 0, 0, tiled=True)
    base = base[:PANELS].transpose(1, 2, 0, 3).reshape(lrows, part, order)

    half = order // 2
    mine = base[0]
    moved = lax.ppermute(mine[:, half:], "row", [(5, 6), (4, 7), (3, 0)])
    first = jnp.concatenate([mine[:, :tile], moved[:, : half - tile]], axis=1)
    packed = jnp.where(my_row >= PANELS, moved, jnp.where(my_row == 0, first, mine[:, :half]))

    cut = child_tiles.reshape(stored, col_count, row_count, deep, tile).transpose(2, 1, 3, 0, 4)
    cut = cut.reshape(devices, deep, stored, tile)
    cut, packed = lax.optimization_barrier((cut, packed))
    spread = lax.all_to_all(cut, BOTH, split_axis=0, concat_axis=0, tiled=True)
    packed = lax.all_gather(packed, BOTH, axis=0, tiled=True)
    places = {(i, j): (i, j) for i in range(PANELS) for j in range(min(i, 2) + 1)}
    places |= {(3, 3): (0, 1), (4, 3): (7, 0), (4, 4): (7, 1)}
    places |= {(5, 3): (6, 0), (5, 4): (6, 1), (5, 5): (6, 2)}

    rows_all = tile_target[:, :, 0].reshape(-1)
    cols_all = tile_target[:, :, 1].reshape(-1)
    owner = rows_all % row_count * col_count + cols_all % col_count
    target = owner * slots + rows_all // row_count * lcols + cols_all // col_count
    tiles = jnp.arange(devices * slots, dtype=jnp.int32)
    hot = (tiles[:, None] == target[None, :]).astype(BF16)
    hot, spread = lax.optimization_barrier((hot, spread))
    sums = child_sum(hot, spread)

    panel = sums.reshape(deep, row_count, col_count, lrows, lcols, tile)[:, :, :PANELS, :, 0]
    panel = panel.transpose(1, 3, 0, 2, 4).reshape(row_count, lrows * deep, order)
    panel = lax.all_to_all(panel, "row", 0, 0, tiled=True)
    panel = panel.reshape(row_count, lrows, deep, order).transpose(1, 0, 2, 3)
    solving = base + panel.reshape(lrows, part, order)

    row_side = lax.all_gather(solving.reshape(lrows * part, order), "col", axis=0, tiled=True)
    row_side = row_side.reshape(col_count, lrows, part, order).transpose(1, 0, 2, 3)
    row_side = row_side.reshape(lrows * tile, order)
    cross = solving.reshape(lrows, row_count, deep, order).transpose(1, 0, 2, 3)
    cross = lax.all_to_all(cross.reshape(row_count, lrows * deep, order), "row", 0, 0, tiled=True)
    cross = cross.reshape(row_count, lcols, stride, deep, order).transpose(2, 0, 1, 3, 4)
    cross = cross.reshape(col_count, lcols * deep, order)
    cross = lax.all_to_all(cross, "col", 0, 0, tiled=True)
    cross, sums = lax.optimization_barrier((cross, sums))
    cross = lax.all_gather(cross.reshape(-1, order), "row", axis=0, tiled=True)
    col_side = cross.reshape(row_count, col_count, lcols, deep, order).transpose(2, 1, 0, 3, 4)
    col_side = col_side.reshape(lcols * tile, order)

    summed = sums.reshape(deep, devices, slots, tile).transpose(1, 0, 2, 3)
    summed = lax.all_to_all(summed, BOTH, split_axis=0, concat_axis=0, tiled=True)

    lower, inverse = factor_leading(packed, places, tile, PANELS)
    row_panel = dot_nt(row_side, inverse)
    col_panel = dot_nt(col_side, inverse)
    update = dot_nt(row_panel, col_panel).reshape(lrows, tile, lcols, tile)

    summed = summed.reshape(row_count, col_count, deep, lrows, lcols, tile)
    summed = summed.transpose(3, 1, 0, 2, 4, 5).reshape(lrows, tile, lcols, tile)
    trailing = front - update + summed

    row_ids = my_row + row_count * jnp.arange(lrows, dtype=jnp.int32)
    col_ids = my_col + col_count * jnp.arange(lcols, dtype=jnp.int32)
    trailing = jnp.where((row_ids < PANELS)[:, None, None, None], jnp.zeros((), F32), trailing)
    k = jnp.minimum(my_col, PANELS - 1)
    below = lax.dynamic_slice_in_dim(row_panel.reshape(lrows, tile, order), k * tile, tile, axis=2)
    top = lax.dynamic_slice(
        lower, (jnp.minimum(my_row, PANELS - 1) * tile, k * tile), (tile, tile)
    )
    factor = jnp.where((row_ids < PANELS)[:, None, None], top[None], below)
    front = jnp.where(
        (col_ids < PANELS)[None, None, :, None], factor[:, :, None, :], trailing
    )
    return front.reshape(parent_front.shape)


def solution(mesh):
    return jax.shard_map(
        shards,
        mesh=mesh,
        in_specs=(
            P(None, "row", None, None, "col", None),
            P(("row", "col"), None, None, None),
            P(),
        ),
        out_specs=P(None, "row", None, None, "col", None),
        check_vma=False,
    )
```

```python
import jax
import jax.numpy as jnp
from jax import lax
from jax.experimental import pallas as pl
from jax.experimental.pallas import tpu as pltpu
from jax.sharding import PartitionSpec as P

PANELS = 6
BOTH = ("row", "col")
F32 = jnp.float32
BF16 = jnp.bfloat16
F16 = jnp.float16
HIGHEST = lax.Precision.HIGHEST
HIGH = lax.Precision.HIGH


NT = (((1,), (1,)), ((), ()))
NN = (((1,), (0,)), ((), ()))


def dot(a, b, dims, precision=HIGHEST):
    return lax.dot_general(a, b, dims, precision=precision, preferred_element_type=F32)


def split(x):
    high = x.astype(BF16)
    return high, (x - high.astype(F32)).astype(BF16)


def dot3(a, b, dims):
    (ah, al), (bh, bl) = split(a), split(b)
    one = lambda p, q: lax.dot_general(p, q, dims, preferred_element_type=F32)
    return one(ah, bh) + (one(ah, bl) + one(al, bh))


def leading_kernel(tile, panels, places, a_ref, l_ref, w_ref, s_ref, acc_ref):
    rows = lax.broadcasted_iota(jnp.int32, (tile, tile), 0)
    cols = lax.broadcasted_iota(jnp.int32, (tile, tile), 1)
    diag = rows == cols
    eye = jnp.where(diag, 1.0, 0.0).astype(F32)
    weight = jnp.where(rows > cols, 1.0, jnp.where(diag, 0.5, 0.0)).astype(F32)

    def at(index):
        return pl.ds(pl.multiple_of(index * tile, tile), tile)

    for (i, j), (down, across) in places.items():
        s_ref[i * tile : (i + 1) * tile, j * tile : (j + 1) * tile] = a_ref[
            down * tile : (down + 1) * tile, across * tile : (across + 1) * tile
        ]
    l_ref[...] = jnp.zeros_like(l_ref)
    w_ref[...] = jnp.zeros_like(w_ref)

    @pl.loop(0, panels)
    def _(k):
        here = at(k)
        block = s_ref[here, here]
        only = jnp.where(diag, block, 0.0)
        down = lax.rsqrt(jnp.sum(only, axis=1, keepdims=True))
        across = lax.rsqrt(jnp.sum(only, axis=0, keepdims=True))
        w_ref[here, here] = jnp.where(diag, down, 0.0)
        acc_ref[...] = block * down * across - eye

        def improve():
            w = w_ref[here, here]
            w_ref[here, here] = w - dot(acc_ref[...] * weight, w, NN)

        def unfinished(state):
            step, worst = state
            return (worst > 1e-5) & (step < 16)

        def refine(state):
            step, _ = state
            improve()
            w = w_ref[here, here]
            left = dot(dot(w, s_ref[here, here], NN), w, NT) - eye
            acc_ref[...] = left
            return step + 1, jnp.max(jnp.abs(left))

        lax.while_loop(unfinished, refine, (jnp.int32(0), jnp.max(jnp.abs(acc_ref[...]))))
        improve()
        l_ref[here, here] = jnp.where(
            rows >= cols, dot(s_ref[here, here], w_ref[here, here], NT), 0.0
        )

        @pl.loop(k + 1, panels)
        def _(i):
            l_ref[at(i), here] = dot3(s_ref[at(i), here], w_ref[here, here], NT)

        @pl.loop(k + 1, panels)
        def _(i):
            @pl.loop(k + 1, i + 1)
            def _(j):
                s_ref[at(i), at(j)] -= dot3(l_ref[at(i), here], l_ref[at(j), here], NT)

    @pl.loop(1, panels)
    def _(i):
        @pl.loop(0, i)
        def _(j):
            acc_ref[...] = jnp.zeros_like(acc_ref)

            @pl.loop(j, i)
            def _(m):
                acc_ref[...] += dot3(l_ref[at(i), at(m)], w_ref[at(m), at(j)], NN)

            w_ref[at(i), at(j)] = -dot3(w_ref[at(i), at(i)], acc_ref[...], NN)


def factor_leading(packed, places, tile, panels):
    order = tile * panels
    whole = pl.BlockSpec(memory_space=pltpu.VMEM)
    return pl.pallas_call(
        lambda *refs: leading_kernel(tile, panels, places, *refs),
        out_shape=[jax.ShapeDtypeStruct((order, order), F32)] * 2,
        in_specs=[whole],
        out_specs=[whole] * 2,
        scratch_shapes=[pltpu.VMEM((order, order), F32), pltpu.VMEM((tile, tile), F32)],
        compiler_params=pltpu.CompilerParams(vmem_limit_bytes=44 << 20),
        cost_estimate=pl.CostEstimate(
            flops=24 * order**3, bytes_accessed=12 * order**2, transcendentals=0
        ),
        name="leading",
    )(packed)


def cut_kernel(child_ref, out_ref, wide_ref):
    pieces, deep, stored, tile = out_ref.shape
    lanes = wide_ref.shape[-1]
    for h in range(tile // lanes):
        across = slice(h * lanes, (h + 1) * lanes)
        wide_ref[h] = child_ref[:, :, across].astype(F32).reshape(wide_ref.shape[1:])
        for d in range(pieces):
            for e in range(deep):
                rows = wide_ref[h, pl.ds(d * deep + e, stored, stride=pieces * deep), :]
                out_ref[d, e, :, across] = rows.astype(BF16)


def cut_rows(child, devices):
    stored, tile, _ = child.shape
    deep = tile // devices
    block = 8
    return pl.pallas_call(
        cut_kernel,
        out_shape=jax.ShapeDtypeStruct((devices, deep, stored, tile), BF16),
        grid=(devices // block,),
        in_specs=[pl.BlockSpec((stored, block * deep, tile), lambda g: (0, g, 0))],
        out_specs=pl.BlockSpec((block, deep, stored, tile), lambda g: (g, 0, 0, 0)),
        scratch_shapes=[pltpu.VMEM((tile // 128, stored * block * deep, 128), F32)],
        compiler_params=pltpu.CompilerParams(vmem_limit_bytes=16 << 20),
        cost_estimate=pl.CostEstimate(
            flops=child.size, bytes_accessed=4 * child.size, transcendentals=0
        ),
        name="cut_rows",
    )(child)


def child_sum_kernel(target_ref, child_ref, out_ref):
    @pl.when(pl.program_id(0) == 0)
    def _():
        out_ref[...] = jnp.zeros_like(out_ref)

    sources, pieces, stored, tile = child_ref.shape
    count = sources * stored
    ids = lax.broadcasted_iota(jnp.int32, (out_ref.shape[0], count), 0)
    hot = jnp.where(ids == target_ref[0], 1.0, 0.0).astype(BF16)
    for e in range(pieces):
        right = child_ref[:, e].reshape(count, tile)
        out_ref[:, e * tile : (e + 1) * tile] += jnp.dot(hot, right, preferred_element_type=F32)


def child_sum(target, child, tiles):
    devices, pieces, stored, tile = child.shape
    block = 8
    return pl.pallas_call(
        child_sum_kernel,
        out_shape=jax.ShapeDtypeStruct((tiles, pieces * tile), F32),
        grid=(devices // block,),
        in_specs=[
            pl.BlockSpec((1, 1, block * stored), lambda g: (g, 0, 0)),
            pl.BlockSpec((block, pieces, stored, tile), lambda g: (g, 0, 0, 0)),
        ],
        out_specs=pl.BlockSpec((tiles, pieces * tile), lambda g: (0, 0)),
        compiler_params=pltpu.CompilerParams(vmem_limit_bytes=24 << 20),
        cost_estimate=pl.CostEstimate(
            flops=2 * tiles * child.size,
            bytes_accessed=2 * child.size + 4 * pieces * tiles * tile,
            transcendentals=0,
        ),
        name="child_sum",
    )(target.reshape(devices // block, 1, block * stored), child)


def shards(parent_front, child_tiles, tile_target):
    lrows = parent_front.shape[0]
    tile = parent_front.shape[2]
    lcols = parent_front.shape[3]
    row_count = lax.axis_size("row")
    col_count = lax.axis_size("col")
    devices = row_count * col_count
    stride = col_count // row_count
    order = PANELS * tile
    part = tile // col_count
    deep = tile // devices
    slots = lrows * lcols
    my_row = lax.axis_index("row")
    my_col = lax.axis_index("col")
    front = parent_front.reshape(lrows, tile, lcols, tile)
    stored = child_tiles.shape[1]

    half = order // 2
    mine = lax.all_to_all(front[0, :, 0, :].reshape(col_count, part, tile), "col", 0, 0, tiled=True)
    mine = mine[:PANELS].transpose(1, 0, 2).reshape(part, order)
    moved = lax.ppermute(mine[:, half:], "row", [(5, 6), (4, 7), (3, 0)])
    first = jnp.concatenate([mine[:, :tile], moved[:, : half - tile]], axis=1)
    packed = jnp.where(my_row >= PANELS, moved, jnp.where(my_row == 0, first, mine[:, :half]))
    places = {(i, j): (i, j) for i in range(PANELS) for j in range(min(i, 2) + 1)}
    places |= {(3, 3): (0, 1), (4, 3): (7, 0), (4, 4): (7, 1)}
    places |= {(5, 3): (6, 0), (5, 4): (6, 1), (5, 5): (6, 2)}

    base = front[:, :, 0, :].reshape(lrows, devices, deep, tile).transpose(1, 0, 2, 3)
    base = base.reshape(devices, lrows * deep, tile)
    cut = cut_rows(child_tiles.reshape(stored, tile, tile), devices)
    cut, packed, base = lax.optimization_barrier((cut, packed, base))
    packed = lax.all_gather(packed, BOTH, axis=0, tiled=True)
    base = lax.all_to_all(base, BOTH, split_axis=0, concat_axis=0, tiled=True)
    spread = lax.all_to_all(cut, BOTH, split_axis=0, concat_axis=0, tiled=True)

    rows_all = tile_target[:, :, 0].reshape(-1)
    cols_all = tile_target[:, :, 1].reshape(-1)
    owner = rows_all % row_count * col_count + cols_all % col_count
    target = owner * slots + rows_all // row_count * lcols + cols_all // col_count
    sums = child_sum(target, spread, devices * slots)

    base = base.reshape(row_count, col_count, lrows, deep, tile)[:, :PANELS]
    panel = sums.reshape(row_count, col_count, lrows, lcols, deep, tile)[:, :PANELS, :, 0]
    pieces = (base + panel).transpose(0, 2, 3, 1, 4).reshape(row_count, lrows, deep, order)
    pieces = pieces.astype(F16)
    to_rows = pieces.reshape(row_count, 1, lrows * deep, order)
    to_rows = jnp.broadcast_to(to_rows, (row_count, col_count, lrows * deep, order))
    to_cols = pieces.reshape(row_count, lcols, stride, deep, order).transpose(2, 0, 1, 3, 4)
    to_cols = to_cols.reshape(1, col_count, lcols * deep, order)
    to_cols = jnp.broadcast_to(to_cols, (row_count, col_count, lcols * deep, order))
    to_owner = sums.reshape(devices, slots, deep * tile).astype(F16)
    to_cols = to_cols.reshape(devices, lcols * deep, order)
    to_rows = to_rows.reshape(devices, lrows * deep, order)
    packed, to_cols, to_rows, to_owner = lax.optimization_barrier(
        (packed, to_cols, to_rows, to_owner)
    )
    lower, inverse = factor_leading(packed, places, tile, PANELS)
    col_side = lax.all_to_all(to_cols, BOTH, split_axis=0, concat_axis=0, tiled=True)
    row_side = lax.all_to_all(to_rows, BOTH, split_axis=0, concat_axis=0, tiled=True)
    to_owner, row_side = lax.optimization_barrier((to_owner, row_side))
    summed = lax.all_to_all(to_owner, BOTH, split_axis=0, concat_axis=0, tiled=True)

    col_side = col_side.reshape(devices, lcols, deep, order).transpose(1, 0, 2, 3)
    col_side = col_side.reshape(lcols * tile, order).astype(F32)
    col_side = dot(dot(col_side, inverse, NT, HIGH), inverse, NN, HIGH)
    k = jnp.minimum(my_col, PANELS - 1) * tile
    leading_col = my_col < PANELS
    own = lax.dynamic_slice(inverse, (k, 0), (tile, order))
    own = jnp.where(leading_col, own, col_side[:tile])
    right = jnp.concatenate([own, col_side[tile:]], axis=0)
    right, row_side, summed = lax.optimization_barrier((right, row_side, summed))
    product = dot(row_side.reshape(devices * lrows * deep, order).astype(F32), right, NT, HIGH)
    product = product.reshape(devices, lrows, deep, lcols, tile)
    summed = summed.reshape(devices, lrows, lcols, deep, tile).transpose(0, 1, 3, 2, 4)
    col_ids = my_col + col_count * jnp.arange(lcols, dtype=jnp.int32)
    factored = (col_ids < PANELS)[:, None]
    change = jnp.where(factored, product, summed.astype(F32) - product)
    change = change.transpose(1, 0, 2, 3, 4).reshape(lrows, tile, lcols, tile)
    result = jnp.where(factored, change, front + change)
    row_ids = my_row + row_count * jnp.arange(lrows, dtype=jnp.int32)
    top = lax.dynamic_slice(lower, (jnp.minimum(my_row, PANELS - 1) * tile, k), (tile, tile))
    top = jnp.where(factored, top[:, None, :], jnp.zeros((), F32))
    result = jnp.where((row_ids < PANELS)[:, None, None, None], top[None], result)
    return result.reshape(parent_front.shape)


def solution(mesh):
    return jax.shard_map(
        shards,
        mesh=mesh,
        in_specs=(
            P(None, "row", None, None, "col", None),
            P(("row", "col"), None, None, None),
            P(),
        ),
        out_specs=P(None, "row", None, None, "col", None),
        check_vma=False,
    )
```

```python
import functools

import jax
import jax.numpy as jnp
from jax import lax
from jax.experimental import pallas as pl
from jax.experimental.pallas import tpu as pltpu
from jax.sharding import PartitionSpec as P

PANELS = 6
BOTH = ("row", "col")
F32 = jnp.float32
BF16 = jnp.bfloat16
F16 = jnp.float16
HIGHEST = lax.Precision.HIGHEST


NT = (((1,), (1,)), ((), ()))
NN = (((1,), (0,)), ((), ()))


def dot(a, b, dims, precision=HIGHEST):
    return lax.dot_general(a, b, dims, precision=precision, preferred_element_type=F32)


def split(x):
    high = x.astype(BF16)
    return high, (x - high.astype(F32)).astype(BF16)


def dot3(a, b, dims):
    (ah, al), (bh, bl) = split(a), split(b)
    one = lambda p, q: lax.dot_general(p, q, dims, preferred_element_type=F32)
    return one(ah, bh) + (one(ah, bl) + one(al, bh))


def tile_at(tile, index):
    return pl.ds(pl.multiple_of(index * tile, tile), tile)


def factor_kernel(tile, panels, a_ref, l_ref, w_ref, s_ref, acc_ref):
    rows = lax.broadcasted_iota(jnp.int32, (tile, tile), 0)
    cols = lax.broadcasted_iota(jnp.int32, (tile, tile), 1)
    diag = rows == cols
    eye = jnp.where(diag, 1.0, 0.0).astype(F32)
    weight = jnp.where(rows > cols, 1.0, jnp.where(diag, 0.5, 0.0)).astype(F32)

    at = functools.partial(tile_at, tile)
    place = 0
    for i in range(panels):
        for j in range(i + 1):
            s_ref[i * tile : (i + 1) * tile, j * tile : (j + 1) * tile] = a_ref[
                :, place * tile : (place + 1) * tile
            ]
            place += 1
    l_ref[...] = jnp.zeros_like(l_ref)

    @pl.loop(0, panels)
    def _(k):
        here = at(k)
        block = s_ref[here, here]
        only = jnp.where(diag, block, 0.0)
        down = lax.rsqrt(jnp.sum(only, axis=1, keepdims=True))
        across = lax.rsqrt(jnp.sum(only, axis=0, keepdims=True))
        w_ref[here, :] = jnp.where(diag, down, 0.0)
        acc_ref[...] = block * down * across - eye

        def improve():
            w = w_ref[here, :]
            w_ref[here, :] = w - dot(acc_ref[...] * weight, w, NN)

        def unfinished(state):
            step, worst = state
            return (worst > 1e-5) & (step < 16)

        def refine(state):
            step, _ = state
            improve()
            w = w_ref[here, :]
            left = dot(dot(w, s_ref[here, here], NN), w, NT) - eye
            acc_ref[...] = left
            return step + 1, jnp.max(jnp.abs(left))

        lax.while_loop(unfinished, refine, (jnp.int32(0), jnp.max(jnp.abs(acc_ref[...]))))
        improve()
        l_ref[here, here] = jnp.where(
            rows >= cols, dot(s_ref[here, here], w_ref[here, :], NT), 0.0
        )

        @pl.loop(k + 1, panels)
        def _(i):
            l_ref[at(i), here] = dot3(s_ref[at(i), here], w_ref[here, :], NT)

        @pl.loop(k + 1, panels)
        def _(i):
            @pl.loop(k + 1, i + 1)
            def _(j):
                s_ref[at(i), at(j)] -= dot3(l_ref[at(i), here], l_ref[at(j), here], NT)


def inverse_kernel(tile, panels, l_ref, d_ref, high_ref, low_ref, w_ref, acc_ref):
    at = functools.partial(tile_at, tile)
    w_ref[...] = jnp.zeros_like(w_ref)

    @pl.loop(0, panels)
    def _(i):
        w_ref[at(i), at(i)] = d_ref[at(i), :]

    @pl.loop(1, panels)
    def _(i):
        @pl.loop(0, i)
        def _(j):
            acc_ref[...] = jnp.zeros_like(acc_ref)

            @pl.loop(j, i)
            def _(m):
                acc_ref[...] += dot3(l_ref[at(i), at(m)], w_ref[at(m), at(j)], NN)

            w_ref[at(i), at(j)] = -dot3(d_ref[at(i), :], acc_ref[...], NN)

    @pl.loop(0, panels)
    def _(i):
        high_ref[at(i), :], low_ref[at(i), :] = split(w_ref[at(i), :])


def factor_leading(packed, tile, panels):
    order = tile * panels
    whole = pl.BlockSpec(memory_space=pltpu.VMEM)
    return pl.pallas_call(
        functools.partial(factor_kernel, tile, panels),
        out_shape=[
            jax.ShapeDtypeStruct((order, order), F32),
            jax.ShapeDtypeStruct((order, tile), F32),
        ],
        in_specs=[whole],
        out_specs=[whole] * 2,
        scratch_shapes=[pltpu.VMEM((order, order), F32), pltpu.VMEM((tile, tile), F32)],
        compiler_params=pltpu.CompilerParams(vmem_limit_bytes=32 << 20),
        cost_estimate=pl.CostEstimate(
            flops=12 * order**3, bytes_accessed=8 * order**2, transcendentals=0
        ),
        name="factor",
    )(packed)


def invert_leading(lower, diagonal):
    order, tile = diagonal.shape
    whole = pl.BlockSpec(memory_space=pltpu.VMEM)
    return pl.pallas_call(
        functools.partial(inverse_kernel, tile, order // tile),
        out_shape=[jax.ShapeDtypeStruct((order, order), BF16)] * 2,
        in_specs=[whole] * 2,
        out_specs=[whole] * 2,
        scratch_shapes=[pltpu.VMEM((order, order), F32), pltpu.VMEM((tile, tile), F32)],
        compiler_params=pltpu.CompilerParams(vmem_limit_bytes=36 << 20),
        cost_estimate=pl.CostEstimate(
            flops=12 * order**3, bytes_accessed=8 * order**2, transcendentals=0
        ),
        name="inverse",
    )(lower, diagonal)


def cut_kernel(child_ref, out_ref, wide_ref):
    pieces, deep, stored, tile = out_ref.shape
    lanes = wide_ref.shape[-1]
    for h in range(tile // lanes):
        across = slice(h * lanes, (h + 1) * lanes)
        wide_ref[h] = child_ref[:, :, across].astype(F32).reshape(wide_ref.shape[1:])
        for d in range(pieces):
            for e in range(deep):
                rows = wide_ref[h, pl.ds(d * deep + e, stored, stride=pieces * deep), :]
                out_ref[d, e, :, across] = rows.astype(BF16)


def cut_rows(child, devices):
    stored, tile, _ = child.shape
    deep = tile // devices
    block = 8
    return pl.pallas_call(
        cut_kernel,
        out_shape=jax.ShapeDtypeStruct((devices, deep, stored, tile), BF16),
        grid=(devices // block,),
        in_specs=[pl.BlockSpec((stored, block * deep, tile), lambda g: (0, g, 0))],
        out_specs=pl.BlockSpec((block, deep, stored, tile), lambda g: (g, 0, 0, 0)),
        scratch_shapes=[pltpu.VMEM((tile // 128, stored * block * deep, 128), F32)],
        compiler_params=pltpu.CompilerParams(vmem_limit_bytes=16 << 20),
        cost_estimate=pl.CostEstimate(
            flops=child.size, bytes_accessed=4 * child.size, transcendentals=0
        ),
        name="cut_rows",
    )(child)


def child_sum_kernel(target_ref, child_ref, out_ref):
    @pl.when(pl.program_id(0) == 0)
    def _():
        out_ref[...] = jnp.zeros_like(out_ref)

    sources, pieces, stored, tile = child_ref.shape
    count = sources * stored
    chunk = 256

    @pl.loop(0, out_ref.shape[0] // chunk)
    def _(m):
        rows = pl.ds(pl.multiple_of(m * chunk, chunk), chunk)
        ids = lax.broadcasted_iota(jnp.int32, (chunk, count), 0) + m * chunk
        hot = jnp.where(ids == target_ref[0], 1.0, 0.0).astype(BF16)
        for e in range(pieces):
            right = child_ref[:, e].reshape(count, tile)
            across = slice(e * tile, (e + 1) * tile)
            out_ref[rows, across] += jnp.dot(hot, right, preferred_element_type=F32)


def child_sum(target, child, tiles):
    devices, pieces, stored, tile = child.shape
    block = 8
    return pl.pallas_call(
        child_sum_kernel,
        out_shape=jax.ShapeDtypeStruct((tiles, pieces * tile), F32),
        grid=(devices // block,),
        in_specs=[
            pl.BlockSpec((1, 1, block * stored), lambda g: (g, 0, 0)),
            pl.BlockSpec((block, pieces, stored, tile), lambda g: (g, 0, 0, 0)),
        ],
        out_specs=pl.BlockSpec((tiles, pieces * tile), lambda g: (0, 0)),
        compiler_params=pltpu.CompilerParams(vmem_limit_bytes=24 << 20),
        cost_estimate=pl.CostEstimate(
            flops=2 * tiles * child.size,
            bytes_accessed=2 * child.size + 4 * pieces * tiles * tile,
            transcendentals=0,
        ),
        name="child_sum",
    )(target.reshape(devices // block, 1, block * stored), child)


def whole_call(kernel, name, out_shape, args, scratch=(), scalars=0, limit=32, flops=0):
    whole = pl.BlockSpec(memory_space=pltpu.VMEM)
    moved = sum(x.size * x.dtype.itemsize for x in [*args, *out_shape])
    return pl.pallas_call(
        kernel,
        out_shape=out_shape,
        in_specs=[pl.BlockSpec(memory_space=pltpu.SMEM)] * scalars
        + [whole] * (len(args) - scalars),
        out_specs=[whole] * len(out_shape),
        scratch_shapes=scratch,
        compiler_params=pltpu.CompilerParams(vmem_limit_bytes=limit << 20),
        cost_estimate=pl.CostEstimate(flops=flops, bytes_accessed=moved, transcendentals=0),
        name=name,
    )(*args)


def pack_kernel(panels, base_ref, packed_ref, turned_ref):
    rows, wide, _ = turned_ref.shape
    tile = base_ref.shape[-1]
    cols = base_ref.shape[0] // rows
    deep = packed_ref.shape[0]
    for r in range(rows):
        for k in range(panels):
            turned_ref[r, :, k * tile : (k + 1) * tile] = base_ref[r * cols + k]
    place = 0
    for i in range(panels):
        for j in range(i + 1):
            for e in range(deep):
                at = e * (wide // deep)
                packed_ref[e : e + 1, place * tile : (place + 1) * tile] = base_ref[
                    i * cols + j, at : at + 1, :
                ]
            place += 1


def encode_kernel(panels, sums_ref, base_ref, rows_ref, cols_ref, x_ref):
    rows, wide, order = base_ref.shape
    tile = order // panels
    cols = rows_ref.shape[0] // rows
    slots = sums_ref.shape[0] // rows_ref.shape[0]
    deep = sums_ref.shape[1] // tile
    lrows = wide // deep
    lanes = 128
    lane = lax.broadcasted_iota(jnp.int32, (wide, lanes), 1)
    for r in range(rows):
        powers = jnp.zeros((wide, lanes), F32)
        for k in range(panels):
            first = (r * cols + k) * slots
            child = [
                sums_ref[first : first + lrows, e * tile : (e + 1) * tile] for e in range(deep)
            ]
            x = base_ref[r, :, k * tile : (k + 1) * tile] + jnp.concatenate(child, axis=0)
            top = jnp.maximum(jnp.max(jnp.abs(x), axis=1, keepdims=True), 1e-30)
            power = jnp.floor(jnp.log(top) * 1.4426950408889634) + 1.0
            coded = jnp.round(x * jnp.exp2(15.0 - power))
            coded = jnp.clip(coded, -32767.0, 32767.0)
            powers = jnp.where(lane == k, power, powers)
            for h in range(tile // lanes):
                x_ref[k * (tile // lanes) + h] = coded[:, h * lanes : (h + 1) * lanes]
        x_ref[order // lanes] = powers
        for g in range(order // lanes + 1):
            across = slice(g * lanes, (g + 1) * lanes)
            piece = x_ref[g].astype(jnp.int32).astype(jnp.int16)
            for c in range(cols):
                rows_ref[r * cols + c, :, across] = piece
            for u in range(cols // rows):
                some = x_ref[g, pl.ds(u, wide // 2, stride=2), :]
                some = some.astype(jnp.int32).astype(jnp.int16)
                for m in range(rows):
                    cols_ref[m * cols + u * rows + r, :, across] = some


def spread_rows(raw_ref, out_ref, source, step, count, target, tile):
    lanes = 128
    each = tile // lanes
    groups = raw_ref.shape[0] - 1
    scale = jnp.exp2(raw_ref[groups, pl.ds(source, count, stride=step), :] - 15.0)
    for g in range(groups):
        k = g // each
        x = raw_ref[g, pl.ds(source, count, stride=step), :] * scale[:, k : k + 1]
        out_ref[g, pl.ds(target, count, stride=2), :] = x


def widen(code_ref, raw_ref):
    lanes = 128
    for g in range(raw_ref.shape[0]):
        piece = code_ref[:, :, g * lanes : (g + 1) * lanes].astype(jnp.int32).astype(F32)
        raw_ref[g] = piece.reshape(raw_ref.shape[1:])


def three(ah, al, bh, bl, dims):
    one = lambda p, q: lax.dot_general(p, q, dims, preferred_element_type=F32)
    return one(ah, bh) + (one(ah, bl) + one(al, bh))


def column_kernel(
    tile, panels, code_ref, wh_ref, wl_ref, gh_ref, gl_ref, raw_ref, nat_ref, xh_ref, xl_ref, acc_ref
):
    at = functools.partial(tile_at, tile)
    devices, pieces, _ = code_ref.shape
    lcols = xh_ref.shape[1] // tile
    each = tile // 128
    widen(code_ref, raw_ref)
    for e in range(pieces // lcols):
        for j in range(lcols):
            spread_rows(raw_ref, nat_ref, e * lcols + j, pieces, devices, j * tile + e, tile)
    for k in range(panels):
        x = jnp.concatenate([nat_ref[k * each + h] for h in range(each)], axis=1)
        xh_ref[k], xl_ref[k] = split(x)

    @pl.loop(0, panels)
    def _(step):
        k = panels - 1 - step
        acc_ref[...] = jnp.zeros_like(acc_ref)

        @pl.loop(0, k + 1)
        def _(j):
            acc_ref[...] += three(
                xh_ref[j], xl_ref[j], wh_ref[at(k), at(j)], wl_ref[at(k), at(j)], NT
            )

        xh_ref[k], xl_ref[k] = split(acc_ref[...])

    @pl.loop(0, panels)
    def _(j):
        acc_ref[...] = jnp.zeros_like(acc_ref)

        @pl.loop(j, panels)
        def _(k):
            acc_ref[...] += three(
                xh_ref[k], xl_ref[k], wh_ref[at(k), at(j)], wl_ref[at(k), at(j)], NN
            )

        gh_ref[:, at(j)], gl_ref[:, at(j)] = split(acc_ref[...])


def final_kernel(
    tile,
    panels,
    where_ref,
    code_ref,
    gh_ref,
    gl_ref,
    wh_ref,
    wl_ref,
    top_ref,
    sums_ref,
    front_ref,
    out_ref,
    raw_ref,
    nat_ref,
    bh_ref,
    bl_ref,
    sum_ref,
    add_ref,
):
    lanes = 128
    each = tile // lanes
    devices, pieces, _ = code_ref.shape
    lrows = out_ref.shape[0] // tile
    lcols = out_ref.shape[1] // tile
    deep = pieces // lrows
    my_row = where_ref[0]
    my_col = where_ref[1]
    row_count = where_ref[2]
    factored = my_col < panels
    widen(code_ref, raw_ref)
    for g in range(deep * each):
        sum_ref[g] = sums_ref[:, :, g * lanes : (g + 1) * lanes].reshape(sum_ref.shape[1:])
    bh_ref[...] = gh_ref[...]
    bl_ref[...] = gl_ref[...]

    @pl.when(factored)
    def _():
        bh_ref[:tile] = wh_ref[...]
        bl_ref[:tile] = wl_ref[...]

    @pl.loop(0, lrows)
    def _(i):
        rows = tile_at(tile, i)
        for e in range(deep):
            spread_rows(raw_ref, nat_ref, e * lrows + i, pieces, devices, e, tile)
            for j in range(lcols):
                for h in range(each):
                    add_ref[j * each + h, pl.ds(e, devices, stride=2), :] = sum_ref[
                        e * each + h, pl.ds(j * lrows + i, devices, stride=lcols * lrows), :
                    ]
        x = jnp.concatenate([nat_ref[g] for g in range(nat_ref.shape[0])], axis=1)
        ah, al = split(x)
        leading = my_row + row_count * i < panels
        for j in range(lcols):
            here = slice(j * tile, (j + 1) * tile)
            product = three(ah, al, bh_ref[here], bl_ref[here], NT)
            child = jnp.concatenate([add_ref[j * each + h] for h in range(each)], axis=1)
            value = front_ref[rows, here] + child - product
            cleared = jnp.zeros_like(value)
            if j == 0:
                value = jnp.where(factored, product, value)
                cleared = jnp.where(factored, top_ref[...], cleared)
            out_ref[rows, here] = jnp.where(leading, cleared, value)


def shards(parent_front, child_tiles, tile_target):
    lrows = parent_front.shape[0]
    tile = parent_front.shape[2]
    lcols = parent_front.shape[3]
    row_count = lax.axis_size("row")
    col_count = lax.axis_size("col")
    devices = row_count * col_count
    order = PANELS * tile
    deep = tile // devices
    slots = lrows * lcols
    lanes = 128
    coded = order + lanes
    my_row = lax.axis_index("row")
    my_col = lax.axis_index("col")
    front = parent_front.reshape(lrows * tile, lcols * tile)
    stored = child_tiles.shape[1]
    shape = jax.ShapeDtypeStruct

    base = front[:, :tile].reshape(lrows, devices, deep, tile).transpose(1, 2, 0, 3)
    base = base.reshape(devices, deep * lrows, tile)
    cut = cut_rows(child_tiles.reshape(stored, tile, tile), devices)
    base = lax.all_to_all(base, BOTH, split_axis=0, concat_axis=0, tiled=True)
    packed, base = whole_call(
        functools.partial(pack_kernel, PANELS),
        "pack",
        [
            shape((deep, PANELS * (PANELS + 1) // 2 * tile), F32),
            shape((row_count, deep * lrows, order), F32),
        ],
        [base],
    )
    cut, packed = lax.optimization_barrier((cut, packed))
    packed = lax.all_gather(packed, BOTH, axis=0, tiled=True)
    spread = lax.all_to_all(cut, BOTH, split_axis=0, concat_axis=0, tiled=True)

    rows_all = tile_target[:, :, 0].reshape(-1)
    cols_all = tile_target[:, :, 1].reshape(-1)
    owner = rows_all % row_count * col_count + cols_all % col_count
    target = owner * slots + cols_all // col_count * lrows + rows_all // row_count
    sums = child_sum(target, spread, devices * slots)

    to_rows, to_cols = whole_call(
        functools.partial(encode_kernel, PANELS),
        "encode",
        [
            shape((devices, deep * lrows, coded), jnp.int16),
            shape((devices, deep * lcols, coded), jnp.int16),
        ],
        [sums, base],
        scratch=[pltpu.VMEM((coded // lanes, deep * lrows, lanes), F32)],
    )
    to_owner = sums.reshape(devices, slots, deep * tile).astype(F16)
    packed, to_cols, to_rows, to_owner = lax.optimization_barrier(
        (packed, to_cols, to_rows, to_owner)
    )
    lower, diagonal = factor_leading(packed, tile, PANELS)
    col_side = lax.all_to_all(to_cols, BOTH, split_axis=0, concat_axis=0, tiled=True)
    col_side, lower, diagonal, to_rows = lax.optimization_barrier(
        (col_side, lower, diagonal, to_rows)
    )
    inverse = invert_leading(lower, diagonal)
    row_side = lax.all_to_all(to_rows, BOTH, split_axis=0, concat_axis=0, tiled=True)
    to_owner, row_side = lax.optimization_barrier((to_owner, row_side))
    summed = lax.all_to_all(to_owner, BOTH, split_axis=0, concat_axis=0, tiled=True)

    groups = order // lanes
    right = whole_call(
        functools.partial(column_kernel, tile, PANELS),
        "column",
        [shape((lcols * tile, order), BF16)] * 2,
        [col_side, *inverse],
        scratch=[
            pltpu.VMEM((groups + 1, lcols * tile, lanes), F32),
            pltpu.VMEM((groups, lcols * tile, lanes), F32),
            pltpu.VMEM((PANELS, lcols * tile, tile), BF16),
            pltpu.VMEM((PANELS, lcols * tile, tile), BF16),
            pltpu.VMEM((lcols * tile, tile), F32),
        ],
        flops=12 * lcols * tile * order**2,
    )
    k = jnp.minimum(my_col, PANELS - 1) * tile
    own = [lax.dynamic_slice(w, (k, 0), (tile, order)) for w in inverse]
    top = lax.dynamic_slice(lower, (jnp.minimum(my_row, PANELS - 1) * tile, k), (tile, tile))
    summed = summed.astype(F32)
    where = jnp.stack([my_row, my_col, jnp.int32(row_count)]).astype(jnp.int32)
    (result,) = whole_call(
        functools.partial(final_kernel, tile, PANELS),
        "final",
        [shape(front.shape, F32)],
        [where, row_side, *right, *own, top, summed, front],
        scratch=[
            pltpu.VMEM((groups + 1, lrows * tile, lanes), F32),
            pltpu.VMEM((groups, tile, lanes), F32),
            pltpu.VMEM((lcols * tile, order), BF16),
            pltpu.VMEM((lcols * tile, order), BF16),
            pltpu.VMEM((deep * tile // lanes, lrows * tile * lcols // deep, lanes), F32),
            pltpu.VMEM((lcols * tile // lanes, tile, lanes), F32),
        ],
        scalars=1,
        limit=40,
        flops=6 * lrows * tile * lcols * tile * order,
    )
    return result.reshape(parent_front.shape)


def solution(mesh):
    return jax.shard_map(
        shards,
        mesh=mesh,
        in_specs=(
            P(None, "row", None, None, "col", None),
            P(("row", "col"), None, None, None),
            P(),
        ),
        out_specs=P(None, "row", None, None, "col", None),
        check_vma=False,
    )
```

```python
import functools

import jax
import jax.numpy as jnp
from jax import lax
from jax.experimental import pallas as pl
from jax.experimental.pallas import tpu as pltpu
from jax.sharding import PartitionSpec as P

PANELS = 6
BOTH = ("row", "col")
F32 = jnp.float32
BF16 = jnp.bfloat16
F16 = jnp.float16
HIGHEST = lax.Precision.HIGHEST


NT = (((1,), (1,)), ((), ()))
NN = (((1,), (0,)), ((), ()))


def dot(a, b, dims, precision=HIGHEST):
    return lax.dot_general(a, b, dims, precision=precision, preferred_element_type=F32)


def split(x):
    high = x.astype(BF16)
    return high, (x - high.astype(F32)).astype(BF16)


def three(ah, al, bh, bl, dims):
    (left,), (right,) = dims[0]
    return lax.dot_general(
        jnp.concatenate([ah, ah, al], axis=left),
        jnp.concatenate([bh, bl, bh], axis=right),
        dims,
        preferred_element_type=F32,
    )


def dot3(a, b, dims):
    return three(*split(a), *split(b), dims)


def tile_at(tile, index):
    return pl.ds(pl.multiple_of(index * tile, tile), tile)


def leading_kernel(
    tile,
    panels,
    places,
    where_ref,
    a_ref,
    high_ref,
    low_ref,
    own_high_ref,
    own_low_ref,
    top_ref,
    l_ref,
    s_ref,
    d_ref,
    acc_ref,
):
    rows = lax.broadcasted_iota(jnp.int32, (tile, tile), 0)
    cols = lax.broadcasted_iota(jnp.int32, (tile, tile), 1)
    diag = rows == cols
    eye = jnp.where(diag, 1.0, 0.0).astype(F32)
    weight = jnp.where(rows > cols, 1.0, jnp.where(diag, 0.5, 0.0)).astype(F32)

    at = functools.partial(tile_at, tile)
    for (i, j), (down, across) in places.items():
        s_ref[i * tile : (i + 1) * tile, j * tile : (j + 1) * tile] = a_ref[
            down * tile : (down + 1) * tile, across * tile : (across + 1) * tile
        ]
    l_ref[...] = jnp.zeros_like(l_ref)

    @pl.loop(0, panels)
    def _(k):
        here = at(k)
        block = s_ref[here, here]
        only = jnp.where(diag, block, 0.0)
        down = lax.rsqrt(jnp.sum(only, axis=1, keepdims=True))
        across = lax.rsqrt(jnp.sum(only, axis=0, keepdims=True))
        d_ref[here, :] = jnp.where(diag, down, 0.0)
        acc_ref[...] = block * down * across - eye

        def improve():
            w = d_ref[here, :]
            d_ref[here, :] = w - dot(acc_ref[...] * weight, w, NN)

        def unfinished(state):
            step, worst = state
            return (worst > 1e-5) & (step < 16)

        def refine(state):
            step, _ = state
            improve()
            w = d_ref[here, :]
            left = dot(dot(w, s_ref[here, here], NN), w, NT) - eye
            acc_ref[...] = left
            return step + 1, jnp.max(jnp.abs(left))

        lax.while_loop(unfinished, refine, (jnp.int32(0), jnp.max(jnp.abs(acc_ref[...]))))
        improve()
        l_ref[here, here] = jnp.where(
            rows >= cols, dot(s_ref[here, here], d_ref[here, :], NT), 0.0
        )

        @pl.loop(k + 1, panels)
        def _(i):
            l_ref[at(i), here] = dot3(s_ref[at(i), here], d_ref[here, :], NT)

        @pl.loop(k + 1, panels)
        def _(i):
            @pl.loop(k + 1, i + 1)
            def _(j):
                s_ref[at(i), at(j)] -= dot3(l_ref[at(i), here], l_ref[at(j), here], NT)

    w_ref = s_ref
    w_ref[...] = jnp.zeros_like(w_ref)

    @pl.loop(0, panels)
    def _(i):
        w_ref[at(i), at(i)] = d_ref[at(i), :]

    @pl.loop(1, panels)
    def _(i):
        @pl.loop(0, i)
        def _(j):
            acc_ref[...] = jnp.zeros_like(acc_ref)

            @pl.loop(j, i)
            def _(m):
                acc_ref[...] += dot3(l_ref[at(i), at(m)], w_ref[at(m), at(j)], NN)

            w_ref[at(i), at(j)] = -dot3(d_ref[at(i), :], acc_ref[...], NN)

    @pl.loop(0, panels)
    def _(i):
        high_ref[at(i), :], low_ref[at(i), :] = split(w_ref[at(i), :])

    r = jnp.minimum(where_ref[0], panels - 1)
    c = jnp.minimum(where_ref[1], panels - 1)
    own_high_ref[...], own_low_ref[...] = split(w_ref[at(c), :])
    top_ref[...] = l_ref[at(r), at(c)]


def cut_kernel(child_ref, out_ref, wide_ref):
    pieces, deep, stored, tile = out_ref.shape
    lanes = wide_ref.shape[-1]
    for h in range(tile // lanes):
        across = slice(h * lanes, (h + 1) * lanes)
        wide_ref[h] = child_ref[:, :, across].astype(F32).reshape(wide_ref.shape[1:])
        for d in range(pieces):
            for e in range(deep):
                rows = wide_ref[h, pl.ds(d * deep + e, stored, stride=pieces * deep), :]
                out_ref[d, e, :, across] = rows.astype(BF16)


def cut_rows(child, devices):
    stored, tile, _ = child.shape
    deep = tile // devices
    block = 8
    return pl.pallas_call(
        cut_kernel,
        out_shape=jax.ShapeDtypeStruct((devices, deep, stored, tile), BF16),
        grid=(devices // block,),
        in_specs=[pl.BlockSpec((stored, block * deep, tile), lambda g: (0, g, 0))],
        out_specs=pl.BlockSpec((block, deep, stored, tile), lambda g: (g, 0, 0, 0)),
        scratch_shapes=[pltpu.VMEM((tile // 128, stored * block * deep, 128), F32)],
        compiler_params=pltpu.CompilerParams(vmem_limit_bytes=58 << 20),
        cost_estimate=pl.CostEstimate(
            flops=child.size, bytes_accessed=4 * child.size, transcendentals=0
        ),
        name="cut_rows",
    )(child)


def child_sum_kernel(target_ref, child_ref, out_ref):
    @pl.when(pl.program_id(0) == 0)
    def _():
        out_ref[...] = jnp.zeros_like(out_ref)

    sources, pieces, stored, tile = child_ref.shape
    count = sources * stored
    ids = lax.broadcasted_iota(jnp.int32, (out_ref.shape[0], count), 0)
    hot = jnp.where(ids == target_ref[0], 1.0, 0.0).astype(BF16)
    for e in range(pieces):
        right = child_ref[:, e].reshape(count, tile)
        out_ref[:, e * tile : (e + 1) * tile] += jnp.dot(hot, right, preferred_element_type=F32)


def child_sum(target, child, tiles):
    devices, pieces, stored, tile = child.shape
    block = 8
    return pl.pallas_call(
        child_sum_kernel,
        out_shape=jax.ShapeDtypeStruct((tiles, pieces * tile), F32),
        grid=(devices // block,),
        in_specs=[
            pl.BlockSpec((1, 1, block * stored), lambda g: (g, 0, 0)),
            pl.BlockSpec((block, pieces, stored, tile), lambda g: (g, 0, 0, 0)),
        ],
        out_specs=pl.BlockSpec((tiles, pieces * tile), lambda g: (0, 0)),
        compiler_params=pltpu.CompilerParams(vmem_limit_bytes=24 << 20),
        cost_estimate=pl.CostEstimate(
            flops=2 * tiles * child.size,
            bytes_accessed=2 * child.size + 4 * pieces * tiles * tile,
            transcendentals=0,
        ),
        name="child_sum",
    )(target.reshape(devices // block, 1, block * stored), child)


def whole_call(kernel, name, out_shape, args, scratch=(), scalars=0, limit=32, flops=0):
    whole = pl.BlockSpec(memory_space=pltpu.VMEM)
    moved = sum(x.size * x.dtype.itemsize for x in [*args, *out_shape])
    return pl.pallas_call(
        kernel,
        out_shape=out_shape,
        in_specs=[pl.BlockSpec(memory_space=pltpu.SMEM)] * scalars
        + [whole] * (len(args) - scalars),
        out_specs=[whole] * len(out_shape),
        scratch_shapes=scratch,
        compiler_params=pltpu.CompilerParams(vmem_limit_bytes=limit << 20),
        cost_estimate=pl.CostEstimate(flops=flops, bytes_accessed=moved, transcendentals=0),
        name=name,
    )(*args)


def encode_kernel(panels, rows, deep, sums_ref, base_ref, out_ref, x_ref):
    devices, wide, tile = base_ref.shape
    cols = devices // rows
    slots = sums_ref.shape[0] // devices
    lrows = wide // deep
    lanes = 128
    each = tile // lanes
    groups = panels * each
    coded = (groups + 1) * lanes
    lane = lax.broadcasted_iota(jnp.int32, (wide, lanes), 1)
    for r in range(rows):
        powers = jnp.zeros((wide, lanes), F32)
        for k in range(panels):
            first = (r * cols + k) * slots
            child = [
                sums_ref[first : first + lrows, e * tile : (e + 1) * tile] for e in range(deep)
            ]
            x = base_ref[r * cols + k] + jnp.concatenate(child, axis=0)
            top = jnp.maximum(jnp.max(jnp.abs(x), axis=1, keepdims=True), 1e-30)
            power = jnp.floor(jnp.log(top) * 1.4426950408889634) + 1.0
            code = jnp.round(x * jnp.exp2(15.0 - power))
            code = jnp.clip(code, -32767.0, 32767.0)
            powers = jnp.where(lane == k, power, powers)
            for h in range(each):
                x_ref[k * each + h] = code[:, h * lanes : (h + 1) * lanes]
        x_ref[groups] = powers
        for g in range(groups + 1):
            across = [slice(n * coded + g * lanes, n * coded + (g + 1) * lanes) for n in range(deep + 1)]
            for e in range(deep):
                piece = x_ref[g, e * lrows : (e + 1) * lrows, :]
                piece = piece.astype(jnp.int32).astype(jnp.int16)
                for c in range(cols):
                    out_ref[r * cols + c, :, across[e]] = piece
            for u in range(cols // rows):
                some = x_ref[g, pl.ds(u, lrows, stride=wide // lrows), :]
                some = some.astype(jnp.int32).astype(jnp.int16)
                for m in range(rows):
                    out_ref[m * cols + u * rows + r, :, across[deep]] = some


def spread_rows(raw_ref, first, out_ref, source, step, count, target, tile):
    lanes = 128
    each = tile // lanes
    groups = out_ref.shape[0]
    scale = jnp.exp2(raw_ref[first + groups, pl.ds(source, count, stride=step), :] - 15.0)
    for g in range(groups):
        k = g // each
        x = raw_ref[first + g, pl.ds(source, count, stride=step), :] * scale[:, k : k + 1]
        out_ref[g, pl.ds(target, count, stride=2), :] = x


def widen(code_ref, first, raw_ref):
    lanes = 128
    for g in range(raw_ref.shape[0]):
        across = slice(first + g * lanes, first + (g + 1) * lanes)
        raw_ref[g] = code_ref[:, :, across].astype(jnp.int32).astype(F32).reshape(raw_ref.shape[1:])


def column_kernel(
    tile, panels, code_ref, wh_ref, wl_ref, gh_ref, gl_ref, raw_ref, nat_ref, xh_ref, xl_ref, acc_ref
):
    at = functools.partial(tile_at, tile)
    devices, pieces, wide = code_ref.shape
    lcols = xh_ref.shape[1] // tile
    each = tile // 128
    widen(code_ref, wide - raw_ref.shape[0] * 128, raw_ref)
    for e in range(pieces // lcols):
        for j in range(lcols):
            spread_rows(raw_ref, 0, nat_ref, e * lcols + j, pieces, devices, j * tile + e, tile)
    for k in range(panels):
        x = jnp.concatenate([nat_ref[k * each + h] for h in range(each)], axis=1)
        xh_ref[k], xl_ref[k] = split(x)

    @pl.loop(0, panels)
    def _(step):
        k = panels - 1 - step
        acc_ref[...] = jnp.zeros_like(acc_ref)

        @pl.loop(0, k + 1)
        def _(j):
            acc_ref[...] += three(
                xh_ref[j], xl_ref[j], wh_ref[at(k), at(j)], wl_ref[at(k), at(j)], NT
            )

        xh_ref[k], xl_ref[k] = split(acc_ref[...])

    @pl.loop(0, panels)
    def _(j):
        acc_ref[...] = jnp.zeros_like(acc_ref)

        @pl.loop(j, panels)
        def _(k):
            acc_ref[...] += three(
                xh_ref[k], xl_ref[k], wh_ref[at(k), at(j)], wl_ref[at(k), at(j)], NN
            )

        gh_ref[:, at(j)], gl_ref[:, at(j)] = split(acc_ref[...])


def final_kernel(
    tile,
    panels,
    where_ref,
    code_ref,
    gh_ref,
    gl_ref,
    wh_ref,
    wl_ref,
    top_ref,
    sums_ref,
    front_ref,
    out_ref,
    raw_ref,
    nat_ref,
    bh_ref,
    bl_ref,
    sum_ref,
    add_ref,
):
    lanes = 128
    each = tile // lanes
    devices, pieces, _ = code_ref.shape
    lrows = out_ref.shape[0] // tile
    lcols = out_ref.shape[1] // tile
    groups = nat_ref.shape[0]
    deep = raw_ref.shape[0] // (groups + 1)
    my_row = where_ref[0]
    my_col = where_ref[1]
    row_count = where_ref[2]
    factored = my_col < panels
    widen(code_ref, 0, raw_ref)
    for g in range(deep * each):
        sum_ref[g] = sums_ref[:, :, g * lanes : (g + 1) * lanes].reshape(sum_ref.shape[1:])
    bh_ref[...] = gh_ref[...]
    bl_ref[...] = gl_ref[...]

    @pl.when(factored)
    def _():
        bh_ref[:tile] = wh_ref[...]
        bl_ref[:tile] = wl_ref[...]

    @pl.loop(0, lrows)
    def _(i):
        rows = tile_at(tile, i)
        for e in range(deep):
            spread_rows(raw_ref, e * (groups + 1), nat_ref, i, pieces, devices, e, tile)
            for j in range(lcols):
                for h in range(each):
                    add_ref[j * each + h, pl.ds(e, devices, stride=2), :] = sum_ref[
                        e * each + h, pl.ds(j * lrows + i, devices, stride=lcols * lrows), :
                    ]
        x = jnp.concatenate([nat_ref[g] for g in range(nat_ref.shape[0])], axis=1)
        ah, al = split(x)
        leading = my_row + row_count * i < panels
        for j in range(lcols):
            here = slice(j * tile, (j + 1) * tile)
            product = three(ah, al, bh_ref[here], bl_ref[here], NT)
            child = jnp.concatenate([add_ref[j * each + h] for h in range(each)], axis=1)
            value = front_ref[rows, here] + child - product
            cleared = jnp.zeros_like(value)
            if j == 0:
                value = jnp.where(factored, product, value)
                cleared = jnp.where(factored, top_ref[...], cleared)
            out_ref[rows, here] = jnp.where(leading, cleared, value)


def shards(parent_front, child_tiles, tile_target):
    lrows = parent_front.shape[0]
    tile = parent_front.shape[2]
    lcols = parent_front.shape[3]
    row_count = lax.axis_size("row")
    col_count = lax.axis_size("col")
    devices = row_count * col_count
    order = PANELS * tile
    half = order // 2
    part = tile // col_count
    deep = tile // devices
    slots = lrows * lcols
    lanes = 128
    groups = order // lanes
    my_row = lax.axis_index("row")
    my_col = lax.axis_index("col")
    where = jnp.stack([my_row, my_col, jnp.int32(row_count)]).astype(jnp.int32)
    stored = child_tiles.shape[1]
    shape = jax.ShapeDtypeStruct

    cut = cut_rows(child_tiles.reshape(stored, tile, tile), devices)

    mine = parent_front[0, 0, :, 0, 0, :].reshape(col_count, part, tile)
    mine = lax.all_to_all(mine, "col", 0, 0, tiled=True)
    mine, cut = lax.optimization_barrier((mine, cut))
    mine = mine[:PANELS].transpose(1, 0, 2).reshape(part, order)
    moved = lax.ppermute(mine[:, half:], "row", [(5, 6), (4, 7), (3, 0)])
    first = jnp.concatenate([mine[:, :tile], moved[:, : half - tile]], axis=1)
    packed = jnp.where(my_row >= PANELS, moved, jnp.where(my_row == 0, first, mine[:, :half]))
    places = {(i, j): (i, j) for i in range(PANELS) for j in range(min(i, 2) + 1)}
    places |= {(3, 3): (0, 1), (4, 3): (7, 0), (4, 4): (7, 1)}
    places |= {(5, 3): (6, 0), (5, 4): (6, 1), (5, 5): (6, 2)}
    cut, packed = lax.optimization_barrier((cut, packed))
    packed = lax.all_gather(packed, BOTH, axis=0, tiled=True)
    spread = lax.all_to_all(cut, BOTH, split_axis=0, concat_axis=0, tiled=True)

    later, _ = lax.optimization_barrier((parent_front, cut))
    base = later[:, 0, :, 0, 0, :].reshape(lrows, devices, deep, tile).transpose(1, 2, 0, 3)
    base = base.reshape(devices, deep * lrows, tile)
    front = later.reshape(lrows * tile, lcols * tile)
    spread, base, front = lax.optimization_barrier((spread, base, front))
    base = lax.all_to_all(base, BOTH, split_axis=0, concat_axis=0, tiled=True)

    rows_all = tile_target[:, :, 0].reshape(-1)
    cols_all = tile_target[:, :, 1].reshape(-1)
    owner = rows_all % row_count * col_count + cols_all % col_count
    target = owner * slots + cols_all // col_count * lrows + rows_all // row_count
    sums = child_sum(target, spread, devices * slots)

    (to_both,) = whole_call(
        functools.partial(encode_kernel, PANELS, row_count, deep),
        "encode",
        [shape((devices, lrows, (deep + 1) * (order + lanes)), jnp.int16)],
        [sums, base],
        scratch=[pltpu.VMEM((groups + 1, deep * lrows, lanes), F32)],
    )
    to_owner = sums.reshape(devices, slots, deep * tile).astype(F16)
    packed, _ = lax.optimization_barrier((packed, to_both))
    both = lax.all_to_all(to_both, BOTH, split_axis=0, concat_axis=0, tiled=True)
    *inverse, own_high, own_low, top = whole_call(
        functools.partial(leading_kernel, tile, PANELS, places),
        "leading",
        [shape((order, order), BF16)] * 2
        + [shape((tile, order), BF16)] * 2
        + [shape((tile, tile), F32)],
        [where, packed],
        scratch=[
            pltpu.VMEM((order, order), F32),
            pltpu.VMEM((order, order), F32),
            pltpu.VMEM((order, tile), F32),
            pltpu.VMEM((tile, tile), F32),
        ],
        scalars=1,
        limit=46,
        flops=24 * order**3,
    )
    to_owner, both, inverse = lax.optimization_barrier((to_owner, both, inverse))
    summed = lax.all_to_all(to_owner, BOTH, split_axis=0, concat_axis=0, tiled=True)

    right = whole_call(
        functools.partial(column_kernel, tile, PANELS),
        "column",
        [shape((lcols * tile, order), BF16)] * 2,
        [both, *inverse],
        scratch=[
            pltpu.VMEM((groups + 1, lcols * tile, lanes), F32),
            pltpu.VMEM((groups, lcols * tile, lanes), F32),
            pltpu.VMEM((PANELS, lcols * tile, tile), BF16),
            pltpu.VMEM((PANELS, lcols * tile, tile), BF16),
            pltpu.VMEM((lcols * tile, tile), F32),
        ],
        limit=36,
        flops=12 * lcols * tile * order**2,
    )
    (result,) = whole_call(
        functools.partial(final_kernel, tile, PANELS),
        "final",
        [shape(front.shape, F32)],
        [where, both, *right, own_high, own_low, top, summed.astype(F32), front],
        scratch=[
            pltpu.VMEM((deep * (groups + 1), devices * lrows, lanes), F32),
            pltpu.VMEM((groups, tile, lanes), F32),
            pltpu.VMEM((lcols * tile, order), BF16),
            pltpu.VMEM((lcols * tile, order), BF16),
            pltpu.VMEM((deep * tile // lanes, devices * slots, lanes), F32),
            pltpu.VMEM((lcols * tile // lanes, tile, lanes), F32),
        ],
        scalars=1,
        limit=40,
        flops=6 * lrows * tile * lcols * tile * order,
    )
    return result.reshape(parent_front.shape)


def solution(mesh):
    return jax.shard_map(
        shards,
        mesh=mesh,
        in_specs=(
            P(None, "row", None, None, "col", None),
            P(("row", "col"), None, None, None),
            P(),
        ),
        out_specs=P(None, "row", None, None, "col", None),
        check_vma=False,
    )
```

```python
import functools

import jax
import jax.numpy as jnp
from jax import lax
from jax.experimental import pallas as pl
from jax.experimental.pallas import tpu as pltpu
from jax.sharding import PartitionSpec as P

PANELS = 6
BOTH = ("row", "col")
F32 = jnp.float32
BF16 = jnp.bfloat16
F16 = jnp.float16
HIGHEST = lax.Precision.HIGHEST


NT = (((1,), (1,)), ((), ()))
NN = (((1,), (0,)), ((), ()))


def dot(a, b, dims, precision=HIGHEST):
    return lax.dot_general(a, b, dims, precision=precision, preferred_element_type=F32)


def split(x):
    high = x.astype(BF16)
    return high, (x - high.astype(F32)).astype(BF16)


def three(ah, al, bh, bl, dims):
    (left,), (right,) = dims[0]
    return lax.dot_general(
        jnp.concatenate([ah, ah, al], axis=left),
        jnp.concatenate([bh, bl, bh], axis=right),
        dims,
        preferred_element_type=F32,
    )


def dot3(a, b, dims):
    return three(*split(a), *split(b), dims)


def tile_at(tile, index):
    return pl.ds(pl.multiple_of(index * tile, tile), tile)


def leading_kernel(
    tile,
    panels,
    places,
    where_ref,
    a_ref,
    high_ref,
    low_ref,
    own_high_ref,
    own_low_ref,
    top_ref,
    l_ref,
    lh_ref,
    ll_ref,
    s_ref,
    d_ref,
    acc_ref,
):
    rows = lax.broadcasted_iota(jnp.int32, (tile, tile), 0)
    cols = lax.broadcasted_iota(jnp.int32, (tile, tile), 1)
    diag = rows == cols
    eye = jnp.where(diag, 1.0, 0.0).astype(F32)
    weight = jnp.where(rows > cols, 1.0, jnp.where(diag, 0.5, 0.0)).astype(F32)

    at = functools.partial(tile_at, tile)
    for (i, j), (down, across) in places.items():
        s_ref[i * tile : (i + 1) * tile, j * tile : (j + 1) * tile] = a_ref[
            down * tile : (down + 1) * tile, across * tile : (across + 1) * tile
        ]
    l_ref[...] = jnp.zeros_like(l_ref)

    @pl.loop(0, panels)
    def _(k):
        here = at(k)
        block = s_ref[here, here]
        only = jnp.where(diag, block, 0.0)
        down = lax.rsqrt(jnp.sum(only, axis=1, keepdims=True))
        across = lax.rsqrt(jnp.sum(only, axis=0, keepdims=True))
        first = block * down * across - eye

        d_ref[here, :] = (eye - first * weight) * across

        def unfinished(state):
            step, worst = state
            return (worst > 1e-5) & (step < 16)

        def refine(state):
            step, _ = state
            w = d_ref[here, :]
            left = dot(dot(w, s_ref[here, here], NN), w, NT) - eye
            d_ref[here, :] = w - dot3(left * weight, w, NN)
            return step + 1, jnp.max(jnp.abs(left))

        lax.while_loop(unfinished, refine, (jnp.int32(0), jnp.float32(1.0)))
        dh, dl = split(d_ref[here, :])
        lower = three(*split(s_ref[here, here]), dh, dl, NT)
        l_ref[here, here] = jnp.where(rows >= cols, lower, 0.0)

        @pl.loop(k + 1, panels)
        def _(i):
            below = three(*split(s_ref[at(i), here]), *split(d_ref[here, :]), NT)
            l_ref[at(i), here] = below
            lh_ref[at(i), here], ll_ref[at(i), here] = split(below)

        @pl.loop(k + 1, panels)
        def _(i):
            @pl.loop(k + 1, i + 1)
            def _(j):
                s_ref[at(i), at(j)] -= three(
                    lh_ref[at(i), here],
                    ll_ref[at(i), here],
                    lh_ref[at(j), here],
                    ll_ref[at(j), here],
                    NT,
                )

    high_ref[...] = jnp.zeros_like(high_ref)
    low_ref[...] = jnp.zeros_like(low_ref)

    @pl.loop(0, panels)
    def _(i):
        high_ref[at(i), at(i)], low_ref[at(i), at(i)] = split(d_ref[at(i), :])

    @pl.loop(1, panels)
    def _(i):
        @pl.loop(0, i)
        def _(j):
            acc_ref[...] = jnp.zeros_like(acc_ref)

            @pl.loop(j, i)
            def _(m):
                acc_ref[...] += three(
                    lh_ref[at(i), at(m)],
                    ll_ref[at(i), at(m)],
                    high_ref[at(m), at(j)],
                    low_ref[at(m), at(j)],
                    NN,
                )

            entry = -three(
                high_ref[at(i), at(i)], low_ref[at(i), at(i)], *split(acc_ref[...]), NN
            )
            high_ref[at(i), at(j)], low_ref[at(i), at(j)] = split(entry)

    r = jnp.minimum(where_ref[0], panels - 1)
    c = jnp.minimum(where_ref[1], panels - 1)
    own_high_ref[...] = high_ref[at(c), :]
    own_low_ref[...] = low_ref[at(c), :]
    top_ref[...] = l_ref[at(r), at(c)]


def cut_kernel(child_ref, out_ref, wide_ref):
    pieces, deep, stored, tile = out_ref.shape
    lanes = wide_ref.shape[-1]
    for h in range(tile // lanes):
        across = slice(h * lanes, (h + 1) * lanes)
        wide_ref[h] = child_ref[:, :, across].astype(F32).reshape(wide_ref.shape[1:])
        for d in range(pieces):
            for e in range(deep):
                rows = wide_ref[h, pl.ds(d * deep + e, stored, stride=pieces * deep), :]
                out_ref[d, e, :, across] = rows.astype(BF16)


def cut_rows(child, devices, share, shares):
    stored, tile, _ = child.shape
    stored = stored // shares
    deep = tile // devices
    block = 8
    return pl.pallas_call(
        cut_kernel,
        out_shape=jax.ShapeDtypeStruct((devices, deep, stored, tile), BF16),
        grid=(devices // block,),
        in_specs=[pl.BlockSpec((stored, block * deep, tile), lambda g: (share, g, 0))],
        out_specs=pl.BlockSpec((block, deep, stored, tile), lambda g: (g, 0, 0, 0)),
        scratch_shapes=[pltpu.VMEM((tile // 128, stored * block * deep, 128), F32)],
        compiler_params=pltpu.CompilerParams(vmem_limit_bytes=58 << 20),
        cost_estimate=pl.CostEstimate(
            flops=child.size // shares, bytes_accessed=4 * child.size // shares, transcendentals=0
        ),
        name="cut_rows",
    )(child)


def child_sum_kernel(target_ref, child_ref, start_ref, out_ref):
    @pl.when(pl.program_id(0) == 0)
    def _():
        out_ref[...] = start_ref[...]

    sources, pieces, stored, tile = child_ref.shape
    count = sources * stored
    ids = lax.broadcasted_iota(jnp.int32, (out_ref.shape[0], count), 0)
    hot = jnp.where(ids == target_ref[0], 1.0, 0.0).astype(BF16)
    for e in range(pieces):
        right = child_ref[:, e].reshape(count, tile)
        out_ref[:, e * tile : (e + 1) * tile] += jnp.dot(hot, right, preferred_element_type=F32)


def child_sum(target, child, start):
    devices, pieces, stored, tile = child.shape
    tiles = start.shape[0]
    block = 512 // stored
    resident = pl.BlockSpec((tiles, pieces * tile), lambda g: (0, 0))
    return pl.pallas_call(
        child_sum_kernel,
        out_shape=jax.ShapeDtypeStruct((tiles, pieces * tile), F32),
        grid=(devices // block,),
        in_specs=[
            pl.BlockSpec((1, 1, block * stored), lambda g: (g, 0, 0)),
            pl.BlockSpec((block, pieces, stored, tile), lambda g: (g, 0, 0, 0)),
            resident,
        ],
        out_specs=resident,
        compiler_params=pltpu.CompilerParams(vmem_limit_bytes=24 << 20),
        cost_estimate=pl.CostEstimate(
            flops=2 * tiles * child.size,
            bytes_accessed=2 * child.size + 8 * pieces * tiles * tile,
            transcendentals=0,
        ),
        name="child_sum",
    )(target.reshape(devices // block, 1, block * stored), child, start)


def whole_call(kernel, name, out_shape, args, scratch=(), scalars=0, limit=58, flops=0):
    whole = pl.BlockSpec(memory_space=pltpu.VMEM)
    moved = sum(x.size * x.dtype.itemsize for x in [*args, *out_shape])
    return pl.pallas_call(
        kernel,
        out_shape=out_shape,
        in_specs=[pl.BlockSpec(memory_space=pltpu.SMEM)] * scalars
        + [whole] * (len(args) - scalars),
        out_specs=[whole] * len(out_shape),
        scratch_shapes=scratch,
        compiler_params=pltpu.CompilerParams(vmem_limit_bytes=limit << 20),
        cost_estimate=pl.CostEstimate(flops=flops, bytes_accessed=moved, transcendentals=0),
        name=name,
    )(*args)


def encode_kernel(panels, rows, deep, sums_ref, base_ref, out_ref, x_ref):
    devices, wide, tile = base_ref.shape
    cols = devices // rows
    slots = sums_ref.shape[0] // devices
    lrows = wide // deep
    lanes = 128
    each = tile // lanes
    groups = panels * each
    coded = (groups + 1) * lanes
    lane = lax.broadcasted_iota(jnp.int32, (wide, lanes), 1)
    for r in range(rows):
        powers = jnp.zeros((wide, lanes), F32)
        for k in range(panels):
            first = (r * cols + k) * slots
            child = [
                sums_ref[first : first + lrows, e * tile : (e + 1) * tile] for e in range(deep)
            ]
            x = base_ref[r * cols + k] + jnp.concatenate(child, axis=0)
            top = jnp.maximum(jnp.max(jnp.abs(x), axis=1, keepdims=True), 1e-30)
            power = jnp.floor(jnp.log(top) * 1.4426950408889634) + 1.0
            code = jnp.round(x * jnp.exp2(15.0 - power))
            code = jnp.clip(code, -32767.0, 32767.0)
            powers = jnp.where(lane == k, power, powers)
            for h in range(each):
                x_ref[k * each + h] = code[:, h * lanes : (h + 1) * lanes]
        x_ref[groups] = powers
        for g in range(groups + 1):
            across = [slice(n * coded + g * lanes, n * coded + (g + 1) * lanes) for n in range(deep + 1)]
            for e in range(deep):
                piece = x_ref[g, e * lrows : (e + 1) * lrows, :]
                piece = piece.astype(jnp.int32).astype(jnp.int16)
                for c in range(cols):
                    out_ref[r * cols + c, :, across[e]] = piece
            for u in range(cols // rows):
                some = x_ref[g, pl.ds(u, lrows, stride=wide // lrows), :]
                some = some.astype(jnp.int32).astype(jnp.int16)
                for m in range(rows):
                    out_ref[m * cols + u * rows + r, :, across[deep]] = some


def spread_rows(raw_ref, first, out_ref, source, step, count, target, tile):
    lanes = 128
    each = tile // lanes
    groups = out_ref.shape[0]
    scale = jnp.exp2(raw_ref[first + groups, pl.ds(source, count, stride=step), :] - 15.0)
    for g in range(groups):
        k = g // each
        x = raw_ref[first + g, pl.ds(source, count, stride=step), :] * scale[:, k : k + 1]
        out_ref[g, pl.ds(target, count, stride=2), :] = x


def widen(code_ref, first, raw_ref):
    lanes = 128
    for g in range(raw_ref.shape[0]):
        across = slice(first + g * lanes, first + (g + 1) * lanes)
        raw_ref[g] = code_ref[:, :, across].astype(jnp.int32).astype(F32).reshape(raw_ref.shape[1:])


def column_kernel(
    tile, panels, code_ref, wh_ref, wl_ref, gh_ref, gl_ref, raw_ref, nat_ref, xh_ref, xl_ref, acc_ref
):
    at = functools.partial(tile_at, tile)
    devices, pieces, wide = code_ref.shape
    lcols = xh_ref.shape[1] // tile
    each = tile // 128
    widen(code_ref, wide - raw_ref.shape[0] * 128, raw_ref)
    for e in range(pieces // lcols):
        for j in range(lcols):
            spread_rows(raw_ref, 0, nat_ref, e * lcols + j, pieces, devices, j * tile + e, tile)
    for k in range(panels):
        x = jnp.concatenate([nat_ref[k * each + h] for h in range(each)], axis=1)
        xh_ref[k], xl_ref[k] = split(x)

    @pl.loop(0, panels)
    def _(step):
        k = panels - 1 - step
        acc_ref[...] = jnp.zeros_like(acc_ref)

        @pl.loop(0, k + 1)
        def _(j):
            acc_ref[...] += three(
                xh_ref[j], xl_ref[j], wh_ref[at(k), at(j)], wl_ref[at(k), at(j)], NT
            )

        xh_ref[k], xl_ref[k] = split(acc_ref[...])

    @pl.loop(0, panels)
    def _(j):
        acc_ref[...] = jnp.zeros_like(acc_ref)

        @pl.loop(j, panels)
        def _(k):
            acc_ref[...] += three(
                xh_ref[k], xl_ref[k], wh_ref[at(k), at(j)], wl_ref[at(k), at(j)], NN
            )

        gh_ref[:, at(j)], gl_ref[:, at(j)] = split(acc_ref[...])


def final_kernel(
    tile,
    panels,
    where_ref,
    code_ref,
    gh_ref,
    gl_ref,
    wh_ref,
    wl_ref,
    top_ref,
    sums_ref,
    front_ref,
    out_ref,
    raw_ref,
    nat_ref,
    bh_ref,
    bl_ref,
    sum_ref,
    add_ref,
):
    lanes = 128
    each = tile // lanes
    devices, pieces, _ = code_ref.shape
    lrows = front_ref.shape[0] // tile
    lcols = front_ref.shape[1] // tile
    groups = nat_ref.shape[0]
    deep = raw_ref.shape[0] // (groups + 1)
    my_row = where_ref[0]
    my_col = where_ref[1]
    row_count = where_ref[2]
    factored = my_col < panels
    widen(code_ref, 0, raw_ref)
    for g in range(deep * each):
        sum_ref[g] = sums_ref[:, :, g * lanes : (g + 1) * lanes].reshape(sum_ref.shape[1:])
    bh_ref[...] = gh_ref[...]
    bl_ref[...] = gl_ref[...]

    @pl.when(factored)
    def _():
        bh_ref[:tile] = wh_ref[...]
        bl_ref[:tile] = wl_ref[...]

    @pl.loop(0, lrows)
    def _(i):
        rows = tile_at(tile, i)
        for e in range(deep):
            spread_rows(raw_ref, e * (groups + 1), nat_ref, i, pieces, devices, e, tile)
            for j in range(lcols):
                for h in range(each):
                    add_ref[j * each + h, pl.ds(e, devices, stride=2), :] = sum_ref[
                        e * each + h, pl.ds(j * lrows + i, devices, stride=lcols * lrows), :
                    ]
        x = jnp.concatenate([nat_ref[g] for g in range(nat_ref.shape[0])], axis=1)
        ah, al = split(x)
        leading = my_row + row_count * i < panels
        for j in range(lcols):
            here = slice(j * tile, (j + 1) * tile)
            product = three(ah, al, bh_ref[here], bl_ref[here], NT)
            child = jnp.concatenate([add_ref[j * each + h] for h in range(each)], axis=1)
            value = front_ref[rows, here] + child - product
            cleared = jnp.zeros_like(value)
            if j == 0:
                value = jnp.where(factored, product, value)
                cleared = jnp.where(factored, top_ref[...], cleared)
            value = jnp.where(leading, cleared, value)
            for h in range(each):
                start = i * (tile * lcols * each) + j * each + h
                out_ref[pl.ds(start, tile, stride=lcols * each), :] = value[
                    :, h * lanes : (h + 1) * lanes
                ]


def shards(parent_front, child_tiles, tile_target):
    lrows = parent_front.shape[0]
    tile = parent_front.shape[2]
    lcols = parent_front.shape[3]
    row_count = lax.axis_size("row")
    col_count = lax.axis_size("col")
    devices = row_count * col_count
    order = PANELS * tile
    half = order // 2
    part = tile // col_count
    deep = tile // devices
    slots = lrows * lcols
    lanes = 128
    groups = order // lanes
    my_row = lax.axis_index("row")
    my_col = lax.axis_index("col")
    where = jnp.stack([my_row, my_col, jnp.int32(row_count)]).astype(jnp.int32)
    stored = child_tiles.shape[1]
    shape = jax.ShapeDtypeStruct

    held = child_tiles.reshape(stored, tile, tile)
    cut = cut_rows(held, devices, 0, 2)

    mine = parent_front[0, 0, :, 0, 0, :].reshape(col_count, part, tile)
    mine = lax.all_to_all(mine, "col", 0, 0, tiled=True)
    mine, cut = lax.optimization_barrier((mine, cut))
    mine = mine[:PANELS].transpose(1, 0, 2).reshape(part, order)
    moved = lax.ppermute(mine[:, half:], "row", [(5, 6), (4, 7), (3, 0)])
    first = jnp.concatenate([mine[:, :tile], moved[:, : half - tile]], axis=1)
    packed = jnp.where(my_row >= PANELS, moved, jnp.where(my_row == 0, first, mine[:, :half]))
    places = {(i, j): (i, j) for i in range(PANELS) for j in range(min(i, 2) + 1)}
    places |= {(3, 3): (0, 1), (4, 3): (7, 0), (4, 4): (7, 1)}
    places |= {(5, 3): (6, 0), (5, 4): (6, 1), (5, 5): (6, 2)}
    cut, packed = lax.optimization_barrier((cut, packed))
    packed = lax.all_gather(packed, BOTH, axis=0, tiled=True)
    spread = lax.all_to_all(cut, BOTH, split_axis=0, concat_axis=0, tiled=True)
    held, _ = lax.optimization_barrier((held, cut))
    cut = cut_rows(held, devices, 1, 2)
    cut, spread = lax.optimization_barrier((cut, spread))
    second = lax.all_to_all(cut, BOTH, split_axis=0, concat_axis=0, tiled=True)

    later, _ = lax.optimization_barrier((parent_front, cut))
    base = later[:, 0, :, 0, 0, :].reshape(lrows, devices, deep, tile).transpose(1, 2, 0, 3)
    base = base.reshape(devices, deep * lrows, tile)
    front = later.reshape(lrows * tile, lcols * tile)
    second, base, front = lax.optimization_barrier((second, base, front))

    rows_all = tile_target[:, :, 0].reshape(-1)
    cols_all = tile_target[:, :, 1].reshape(-1)
    owner = rows_all % row_count * col_count + cols_all % col_count
    target = owner * slots + cols_all // col_count * lrows + rows_all // row_count
    target = target.reshape(devices, stored)
    sums = jnp.zeros((devices * slots, deep * tile), F32)
    sums = child_sum(target[:, : stored // 2], spread, sums)
    second, sums, base = lax.optimization_barrier((second, sums, base))
    base = lax.all_to_all(base, BOTH, split_axis=0, concat_axis=0, tiled=True)
    sums = child_sum(target[:, stored // 2 :], second, sums)

    (to_both,) = whole_call(
        functools.partial(encode_kernel, PANELS, row_count, deep),
        "encode",
        [shape((devices, lrows, (deep + 1) * (order + lanes)), jnp.int16)],
        [sums, base],
        scratch=[pltpu.VMEM((groups + 1, deep * lrows, lanes), F32)],
    )
    to_owner = sums.reshape(devices, slots, deep * tile).astype(F16)
    packed, _ = lax.optimization_barrier((packed, to_both))
    both = lax.all_to_all(to_both, BOTH, split_axis=0, concat_axis=0, tiled=True)
    *inverse, own_high, own_low, top = whole_call(
        functools.partial(leading_kernel, tile, PANELS, places),
        "leading",
        [shape((order, order), BF16)] * 2
        + [shape((tile, order), BF16)] * 2
        + [shape((tile, tile), F32)],
        [where, packed],
        scratch=[
            pltpu.VMEM((order, order), F32),
            pltpu.VMEM((order, order), BF16),
            pltpu.VMEM((order, order), BF16),
            pltpu.VMEM((order, order), F32),
            pltpu.VMEM((order, tile), F32),
            pltpu.VMEM((tile, tile), F32),
        ],
        scalars=1,
        limit=58,
        flops=24 * order**3,
    )
    to_owner, both, top = lax.optimization_barrier((to_owner, both, top))
    summed = lax.all_to_all(to_owner, BOTH, split_axis=0, concat_axis=0, tiled=True)

    right = whole_call(
        functools.partial(column_kernel, tile, PANELS),
        "column",
        [shape((lcols * tile, order), BF16)] * 2,
        [both, *inverse],
        scratch=[
            pltpu.VMEM((groups + 1, lcols * tile, lanes), F32),
            pltpu.VMEM((groups, lcols * tile, lanes), F32),
            pltpu.VMEM((PANELS, lcols * tile, tile), BF16),
            pltpu.VMEM((PANELS, lcols * tile, tile), BF16),
            pltpu.VMEM((lcols * tile, tile), F32),
        ],
        limit=58,
        flops=12 * lcols * tile * order**2,
    )
    (result,) = whole_call(
        functools.partial(final_kernel, tile, PANELS),
        "final",
        [shape((front.size // lanes, lanes), F32)],
        [where, both, *right, own_high, own_low, top, summed.astype(F32), front],
        scratch=[
            pltpu.VMEM((deep * (groups + 1), devices * lrows, lanes), F32),
            pltpu.VMEM((groups, tile, lanes), F32),
            pltpu.VMEM((lcols * tile, order), BF16),
            pltpu.VMEM((lcols * tile, order), BF16),
            pltpu.VMEM((deep * tile // lanes, devices * slots, lanes), F32),
            pltpu.VMEM((lcols * tile // lanes, tile, lanes), F32),
        ],
        scalars=1,
        limit=58,
        flops=6 * lrows * tile * lcols * tile * order,
    )
    return result.reshape(parent_front.shape)


def solution(mesh):
    return jax.shard_map(
        shards,
        mesh=mesh,
        in_specs=(
            P(None, "row", None, None, "col", None),
            P(("row", "col"), None, None, None),
            P(),
        ),
        out_specs=P(None, "row", None, None, "col", None),
        check_vma=False,
    )
```

```python
import functools

import jax
import jax.numpy as jnp
from jax import lax
from jax.experimental import pallas as pl
from jax.experimental.pallas import tpu as pltpu
from jax.sharding import PartitionSpec as P

PANELS = 6
BOTH = ("row", "col")
F32 = jnp.float32
BF16 = jnp.bfloat16
F16 = jnp.float16
HIGHEST = lax.Precision.HIGHEST


NT = (((1,), (1,)), ((), ()))
NN = (((1,), (0,)), ((), ()))


def dot(a, b, dims, precision=HIGHEST):
    return lax.dot_general(a, b, dims, precision=precision, preferred_element_type=F32)


def split(x):
    high = x.astype(BF16)
    return high, (x - high.astype(F32)).astype(BF16)


def three(ah, al, bh, bl, dims):
    (left,), (right,) = dims[0]
    return lax.dot_general(
        jnp.concatenate([ah, ah, al], axis=left),
        jnp.concatenate([bh, bl, bh], axis=right),
        dims,
        preferred_element_type=F32,
    )


def dot3(a, b, dims):
    return three(*split(a), *split(b), dims)


def tile_at(tile, index):
    return pl.ds(pl.multiple_of(index * tile, tile), tile)


def leading_kernel(
    tile,
    panels,
    places,
    where_ref,
    a_ref,
    high_ref,
    low_ref,
    own_high_ref,
    own_low_ref,
    top_ref,
    l_ref,
    lh_ref,
    ll_ref,
    s_ref,
    d_ref,
    acc_ref,
):
    rows = lax.broadcasted_iota(jnp.int32, (tile, tile), 0)
    cols = lax.broadcasted_iota(jnp.int32, (tile, tile), 1)
    diag = rows == cols
    eye = jnp.where(diag, 1.0, 0.0).astype(F32)
    weight = jnp.where(rows > cols, 1.0, jnp.where(diag, 0.5, 0.0)).astype(F32)

    at = functools.partial(tile_at, tile)
    for (i, j), (down, across) in places.items():
        s_ref[i * tile : (i + 1) * tile, j * tile : (j + 1) * tile] = a_ref[
            down * tile : (down + 1) * tile, across * tile : (across + 1) * tile
        ]
    l_ref[...] = jnp.zeros_like(l_ref)

    @pl.loop(0, panels)
    def _(k):
        here = at(k)
        block = s_ref[here, here]
        only = jnp.where(diag, block, 0.0)
        down = lax.rsqrt(jnp.sum(only, axis=1, keepdims=True))
        across = lax.rsqrt(jnp.sum(only, axis=0, keepdims=True))
        first = block * down * across - eye

        d_ref[here, :] = (eye - first * weight) * across

        def unfinished(state):
            step, worst = state
            return (worst > 1e-5) & (step < 16)

        def refine(state):
            step, _ = state
            w = d_ref[here, :]
            left = dot(dot(w, s_ref[here, here], NN), w, NT) - eye
            d_ref[here, :] = w - dot3(left * weight, w, NN)
            return step + 1, jnp.max(jnp.abs(left))

        lax.while_loop(unfinished, refine, (jnp.int32(0), jnp.float32(1.0)))
        dh, dl = split(d_ref[here, :])
        lower = three(*split(s_ref[here, here]), dh, dl, NT)
        l_ref[here, here] = jnp.where(rows >= cols, lower, 0.0)

        @pl.loop(k + 1, panels)
        def _(i):
            below = three(*split(s_ref[at(i), here]), *split(d_ref[here, :]), NT)
            l_ref[at(i), here] = below
            lh_ref[at(i), here], ll_ref[at(i), here] = split(below)

        @pl.loop(k + 1, panels)
        def _(i):
            @pl.loop(k + 1, i + 1)
            def _(j):
                s_ref[at(i), at(j)] -= three(
                    lh_ref[at(i), here],
                    ll_ref[at(i), here],
                    lh_ref[at(j), here],
                    ll_ref[at(j), here],
                    NT,
                )

    high_ref[...] = jnp.zeros_like(high_ref)
    low_ref[...] = jnp.zeros_like(low_ref)

    @pl.loop(0, panels)
    def _(i):
        high_ref[at(i), at(i)], low_ref[at(i), at(i)] = split(d_ref[at(i), :])

    @pl.loop(1, panels)
    def _(i):
        @pl.loop(0, i)
        def _(j):
            acc_ref[...] = jnp.zeros_like(acc_ref)

            @pl.loop(j, i)
            def _(m):
                acc_ref[...] += three(
                    lh_ref[at(i), at(m)],
                    ll_ref[at(i), at(m)],
                    high_ref[at(m), at(j)],
                    low_ref[at(m), at(j)],
                    NN,
                )

            entry = -three(
                high_ref[at(i), at(i)], low_ref[at(i), at(i)], *split(acc_ref[...]), NN
            )
            high_ref[at(i), at(j)], low_ref[at(i), at(j)] = split(entry)

    r = jnp.minimum(where_ref[0], panels - 1)
    c = jnp.minimum(where_ref[1], panels - 1)
    own_high_ref[...] = high_ref[at(c), :]
    own_low_ref[...] = low_ref[at(c), :]
    top_ref[...] = l_ref[at(r), at(c)]


def cut_kernel(child_ref, out_ref, wide_ref):
    pieces, deep, stored, tile = out_ref.shape
    lanes = wide_ref.shape[-1]
    for h in range(tile // lanes):
        across = slice(h * lanes, (h + 1) * lanes)
        wide_ref[h] = child_ref[:, :, across].astype(F32).reshape(wide_ref.shape[1:])
        for d in range(pieces):
            for e in range(deep):
                rows = wide_ref[h, pl.ds(d * deep + e, stored, stride=pieces * deep), :]
                out_ref[d, e, :, across] = rows.astype(BF16)


def cut_rows(child, devices):
    stored, tile, _ = child.shape
    deep = tile // devices
    block = 16
    return pl.pallas_call(
        cut_kernel,
        out_shape=jax.ShapeDtypeStruct((devices, deep, stored, tile), BF16),
        grid=(devices // block,),
        in_specs=[pl.BlockSpec((stored, block * deep, tile), lambda g: (0, g, 0))],
        out_specs=pl.BlockSpec((block, deep, stored, tile), lambda g: (g, 0, 0, 0)),
        scratch_shapes=[pltpu.VMEM((tile // 128, stored * block * deep, 128), F32)],
        compiler_params=pltpu.CompilerParams(vmem_limit_bytes=58 << 20),
        cost_estimate=pl.CostEstimate(
            flops=child.size, bytes_accessed=4 * child.size, transcendentals=0
        ),
        name="cut_rows",
    )(child)


def child_sum_kernel(target_ref, child_ref, out_ref):
    @pl.when(pl.program_id(0) == 0)
    def _():
        out_ref[...] = jnp.zeros_like(out_ref)

    sources, pieces, stored, tile = child_ref.shape
    count = sources * stored
    ids = lax.broadcasted_iota(jnp.int32, (out_ref.shape[0], count), 0)
    hot = jnp.where(ids == target_ref[0], 1.0, 0.0).astype(BF16)
    for e in range(pieces):
        right = child_ref[:, e].reshape(count, tile)
        out_ref[:, e * tile : (e + 1) * tile] += jnp.dot(hot, right, preferred_element_type=F32)


def child_sum(target, child, tiles):
    devices, pieces, stored, tile = child.shape
    block = 512 // stored
    return pl.pallas_call(
        child_sum_kernel,
        out_shape=jax.ShapeDtypeStruct((tiles, pieces * tile), F32),
        grid=(devices // block,),
        in_specs=[
            pl.BlockSpec((1, 1, block * stored), lambda g: (g, 0, 0)),
            pl.BlockSpec((block, pieces, stored, tile), lambda g: (g, 0, 0, 0)),
        ],
        out_specs=pl.BlockSpec((tiles, pieces * tile), lambda g: (0, 0)),
        compiler_params=pltpu.CompilerParams(vmem_limit_bytes=24 << 20),
        cost_estimate=pl.CostEstimate(
            flops=2 * tiles * child.size,
            bytes_accessed=2 * child.size + 4 * pieces * tiles * tile,
            transcendentals=0,
        ),
        name="child_sum",
    )(target.reshape(devices // block, 1, block * stored), child)


def whole_call(kernel, name, out_shape, args, scratch=(), scalars=0, limit=58, flops=0):
    whole = pl.BlockSpec(memory_space=pltpu.VMEM)
    moved = sum(x.size * x.dtype.itemsize for x in [*args, *out_shape])
    return pl.pallas_call(
        kernel,
        out_shape=out_shape,
        in_specs=[pl.BlockSpec(memory_space=pltpu.SMEM)] * scalars
        + [whole] * (len(args) - scalars),
        out_specs=[whole] * len(out_shape),
        scratch_shapes=scratch,
        compiler_params=pltpu.CompilerParams(vmem_limit_bytes=limit << 20),
        cost_estimate=pl.CostEstimate(flops=flops, bytes_accessed=moved, transcendentals=0),
        name=name,
    )(*args)


def encode_kernel(panels, rows, deep, sums_ref, base_ref, out_ref, x_ref):
    devices, wide, tile = base_ref.shape
    cols = devices // rows
    slots = sums_ref.shape[0] // devices
    lrows = wide // deep
    lanes = 128
    each = tile // lanes
    groups = panels * each
    coded = (groups + 1) * lanes
    lane = lax.broadcasted_iota(jnp.int32, (wide, lanes), 1)
    for r in range(rows):
        powers = jnp.zeros((wide, lanes), F32)
        for k in range(panels):
            first = (r * cols + k) * slots
            child = [
                sums_ref[first : first + lrows, e * tile : (e + 1) * tile] for e in range(deep)
            ]
            x = base_ref[r * cols + k] + jnp.concatenate(child, axis=0)
            top = jnp.maximum(jnp.max(jnp.abs(x), axis=1, keepdims=True), 1e-30)
            power = jnp.floor(jnp.log(top) * 1.4426950408889634) + 1.0
            code = jnp.round(x * jnp.exp2(15.0 - power))
            code = jnp.clip(code, -32767.0, 32767.0)
            powers = jnp.where(lane == k, power, powers)
            for h in range(each):
                x_ref[k * each + h] = code[:, h * lanes : (h + 1) * lanes]
        x_ref[groups] = powers
        for g in range(groups + 1):
            across = [slice(n * coded + g * lanes, n * coded + (g + 1) * lanes) for n in range(deep + 1)]
            for e in range(deep):
                piece = x_ref[g, e * lrows : (e + 1) * lrows, :]
                piece = piece.astype(jnp.int32).astype(jnp.int16)
                for c in range(cols):
                    out_ref[r * cols + c, :, across[e]] = piece
            for u in range(cols // rows):
                some = x_ref[g, pl.ds(u, lrows, stride=wide // lrows), :]
                some = some.astype(jnp.int32).astype(jnp.int16)
                for m in range(rows):
                    out_ref[m * cols + u * rows + r, :, across[deep]] = some


def spread_rows(raw_ref, first, out_ref, source, step, count, target, tile):
    lanes = 128
    each = tile // lanes
    groups = out_ref.shape[0]
    scale = jnp.exp2(raw_ref[first + groups, pl.ds(source, count, stride=step), :] - 15.0)
    for g in range(groups):
        k = g // each
        x = raw_ref[first + g, pl.ds(source, count, stride=step), :] * scale[:, k : k + 1]
        out_ref[g, pl.ds(target, count, stride=2), :] = x


def widen(code_ref, first, raw_ref):
    lanes = 128
    for g in range(raw_ref.shape[0]):
        across = slice(first + g * lanes, first + (g + 1) * lanes)
        raw_ref[g] = code_ref[:, :, across].astype(jnp.int32).astype(F32).reshape(raw_ref.shape[1:])


def column_kernel(
    tile, panels, code_ref, wh_ref, wl_ref, gh_ref, gl_ref, raw_ref, nat_ref, xh_ref, xl_ref, acc_ref
):
    at = functools.partial(tile_at, tile)
    devices, pieces, wide = code_ref.shape
    lcols = xh_ref.shape[1] // tile
    each = tile // 128
    widen(code_ref, wide - raw_ref.shape[0] * 128, raw_ref)
    for e in range(pieces // lcols):
        for j in range(lcols):
            spread_rows(raw_ref, 0, nat_ref, e * lcols + j, pieces, devices, j * tile + e, tile)
    for k in range(panels):
        x = jnp.concatenate([nat_ref[k * each + h] for h in range(each)], axis=1)
        xh_ref[k], xl_ref[k] = split(x)

    @pl.loop(0, panels)
    def _(step):
        k = panels - 1 - step
        acc_ref[...] = jnp.zeros_like(acc_ref)

        @pl.loop(0, k + 1)
        def _(j):
            acc_ref[...] += three(
                xh_ref[j], xl_ref[j], wh_ref[at(k), at(j)], wl_ref[at(k), at(j)], NT
            )

        xh_ref[k], xl_ref[k] = split(acc_ref[...])

    @pl.loop(0, panels)
    def _(j):
        acc_ref[...] = jnp.zeros_like(acc_ref)

        @pl.loop(j, panels)
        def _(k):
            acc_ref[...] += three(
                xh_ref[k], xl_ref[k], wh_ref[at(k), at(j)], wl_ref[at(k), at(j)], NN
            )

        gh_ref[:, at(j)], gl_ref[:, at(j)] = split(acc_ref[...])


def final_kernel(
    tile,
    panels,
    where_ref,
    code_ref,
    gh_ref,
    gl_ref,
    wh_ref,
    wl_ref,
    top_ref,
    sums_ref,
    front_ref,
    out_ref,
    raw_ref,
    nat_ref,
    bh_ref,
    bl_ref,
    sum_ref,
    add_ref,
):
    lanes = 128
    each = tile // lanes
    devices, pieces, _ = code_ref.shape
    lrows = front_ref.shape[0] // tile
    lcols = front_ref.shape[1] // tile
    groups = nat_ref.shape[0]
    deep = raw_ref.shape[0] // (groups + 1)
    my_row = where_ref[0]
    my_col = where_ref[1]
    row_count = where_ref[2]
    factored = my_col < panels
    widen(code_ref, 0, raw_ref)
    for g in range(deep * each):
        sum_ref[g] = sums_ref[:, :, g * lanes : (g + 1) * lanes].reshape(sum_ref.shape[1:])
    bh_ref[...] = gh_ref[...]
    bl_ref[...] = gl_ref[...]

    @pl.when(factored)
    def _():
        bh_ref[:tile] = wh_ref[...]
        bl_ref[:tile] = wl_ref[...]

    @pl.loop(0, lrows)
    def _(i):
        rows = tile_at(tile, i)
        for e in range(deep):
            spread_rows(raw_ref, e * (groups + 1), nat_ref, i, pieces, devices, e, tile)
            for j in range(lcols):
                for h in range(each):
                    add_ref[j * each + h, pl.ds(e, devices, stride=2), :] = sum_ref[
                        e * each + h, pl.ds(j * lrows + i, devices, stride=lcols * lrows), :
                    ]
        x = jnp.concatenate([nat_ref[g] for g in range(nat_ref.shape[0])], axis=1)
        ah, al = split(x)
        leading = my_row + row_count * i < panels
        for j in range(lcols):
            here = slice(j * tile, (j + 1) * tile)
            product = three(ah, al, bh_ref[here], bl_ref[here], NT)
            child = jnp.concatenate([add_ref[j * each + h] for h in range(each)], axis=1)
            value = front_ref[rows, here] + child - product
            cleared = jnp.zeros_like(value)
            if j == 0:
                value = jnp.where(factored, product, value)
                cleared = jnp.where(factored, top_ref[...], cleared)
            value = jnp.where(leading, cleared, value)
            for h in range(each):
                start = i * (tile * lcols * each) + j * each + h
                out_ref[pl.ds(start, tile, stride=lcols * each), :] = value[
                    :, h * lanes : (h + 1) * lanes
                ]


def shards(parent_front, child_tiles, tile_target):
    lrows = parent_front.shape[0]
    tile = parent_front.shape[2]
    lcols = parent_front.shape[3]
    row_count = lax.axis_size("row")
    col_count = lax.axis_size("col")
    devices = row_count * col_count
    order = PANELS * tile
    half = order // 2
    part = tile // col_count
    deep = tile // devices
    slots = lrows * lcols
    lanes = 128
    groups = order // lanes
    my_row = lax.axis_index("row")
    my_col = lax.axis_index("col")
    where = jnp.stack([my_row, my_col, jnp.int32(row_count)]).astype(jnp.int32)
    stored = child_tiles.shape[1]
    shape = jax.ShapeDtypeStruct

    held = child_tiles.reshape(stored, tile, tile)
    cut = cut_rows(held, devices)

    mine = parent_front[0, 0, :, 0, 0, :].reshape(col_count, part, tile)
    mine = lax.all_to_all(mine, "col", 0, 0, tiled=True)
    mine, cut = lax.optimization_barrier((mine, cut))
    mine = mine[:PANELS].transpose(1, 0, 2).reshape(part, order)
    moved = lax.ppermute(mine[:, half:], "row", [(5, 6), (4, 7), (3, 0)])
    first = jnp.concatenate([mine[:, :tile], moved[:, : half - tile]], axis=1)
    packed = jnp.where(my_row >= PANELS, moved, jnp.where(my_row == 0, first, mine[:, :half]))
    places = {(i, j): (i, j) for i in range(PANELS) for j in range(min(i, 2) + 1)}
    places |= {(3, 3): (0, 1), (4, 3): (7, 0), (4, 4): (7, 1)}
    places |= {(5, 3): (6, 0), (5, 4): (6, 1), (5, 5): (6, 2)}
    cut, packed = lax.optimization_barrier((cut, packed))
    packed = lax.all_gather(packed, BOTH, axis=0, tiled=True)
    spread = lax.all_to_all(cut, BOTH, split_axis=0, concat_axis=0, tiled=True)
    later, _ = lax.optimization_barrier((parent_front, cut))
    base = later[:, 0, :, 0, 0, :].reshape(lrows, devices, deep, tile).transpose(1, 2, 0, 3)
    base = base.reshape(devices, deep * lrows, tile)
    front = later.reshape(lrows * tile, lcols * tile)
    spread, base, front = lax.optimization_barrier((spread, base, front))

    rows_all = tile_target[:, :, 0].reshape(-1)
    cols_all = tile_target[:, :, 1].reshape(-1)
    owner = rows_all % row_count * col_count + cols_all % col_count
    target = owner * slots + cols_all // col_count * lrows + rows_all // row_count
    base = lax.all_to_all(base, BOTH, split_axis=0, concat_axis=0, tiled=True)
    sums = child_sum(target, spread, devices * slots)

    (to_both,) = whole_call(
        functools.partial(encode_kernel, PANELS, row_count, deep),
        "encode",
        [shape((devices, lrows, (deep + 1) * (order + lanes)), jnp.int16)],
        [sums, base],
        scratch=[pltpu.VMEM((groups + 1, deep * lrows, lanes), F32)],
        limit=32,
    )
    to_owner = sums.reshape(devices, slots, deep * tile).astype(F16)
    packed, _ = lax.optimization_barrier((packed, to_both))
    both = lax.all_to_all(to_both, BOTH, split_axis=0, concat_axis=0, tiled=True)
    *inverse, own_high, own_low, top = whole_call(
        functools.partial(leading_kernel, tile, PANELS, places),
        "leading",
        [shape((order, order), BF16)] * 2
        + [shape((tile, order), BF16)] * 2
        + [shape((tile, tile), F32)],
        [where, packed],
        scratch=[
            pltpu.VMEM((order, order), F32),
            pltpu.VMEM((order, order), BF16),
            pltpu.VMEM((order, order), BF16),
            pltpu.VMEM((order, order), F32),
            pltpu.VMEM((order, tile), F32),
            pltpu.VMEM((tile, tile), F32),
        ],
        scalars=1,
        limit=58,
        flops=24 * order**3,
    )
    to_owner, both, top = lax.optimization_barrier((to_owner, both, top))
    summed = lax.all_to_all(to_owner, BOTH, split_axis=0, concat_axis=0, tiled=True)

    right = whole_call(
        functools.partial(column_kernel, tile, PANELS),
        "column",
        [shape((lcols * tile, order), BF16)] * 2,
        [both, *inverse],
        scratch=[
            pltpu.VMEM((groups + 1, lcols * tile, lanes), F32),
            pltpu.VMEM((groups, lcols * tile, lanes), F32),
            pltpu.VMEM((PANELS, lcols * tile, tile), BF16),
            pltpu.VMEM((PANELS, lcols * tile, tile), BF16),
            pltpu.VMEM((lcols * tile, tile), F32),
        ],
        limit=58,
        flops=12 * lcols * tile * order**2,
    )
    (result,) = whole_call(
        functools.partial(final_kernel, tile, PANELS),
        "final",
        [shape((front.size // lanes, lanes), F32)],
        [where, both, *right, own_high, own_low, top, summed.astype(F32), front],
        scratch=[
            pltpu.VMEM((deep * (groups + 1), devices * lrows, lanes), F32),
            pltpu.VMEM((groups, tile, lanes), F32),
            pltpu.VMEM((lcols * tile, order), BF16),
            pltpu.VMEM((lcols * tile, order), BF16),
            pltpu.VMEM((deep * tile // lanes, devices * slots, lanes), F32),
            pltpu.VMEM((lcols * tile // lanes, tile, lanes), F32),
        ],
        scalars=1,
        limit=58,
        flops=6 * lrows * tile * lcols * tile * order,
    )
    return result.reshape(parent_front.shape)


def solution(mesh):
    return jax.shard_map(
        shards,
        mesh=mesh,
        in_specs=(
            P(None, "row", None, None, "col", None),
            P(("row", "col"), None, None, None),
            P(),
        ),
        out_specs=P(None, "row", None, None, "col", None),
        check_vma=False,
    )
```

```python
import functools

import jax
import jax.numpy as jnp
from jax import lax
from jax.experimental import pallas as pl
from jax.experimental.pallas import tpu as pltpu
from jax.sharding import PartitionSpec as P

PANELS = 6
BOTH = ("row", "col")
F32 = jnp.float32
BF16 = jnp.bfloat16
F16 = jnp.float16
HIGHEST = lax.Precision.HIGHEST


NT = (((1,), (1,)), ((), ()))
NN = (((1,), (0,)), ((), ()))


def dot(a, b, dims, precision=HIGHEST):
    return lax.dot_general(a, b, dims, precision=precision, preferred_element_type=F32)


def split(x):
    high = x.astype(BF16)
    return high, (x - high.astype(F32)).astype(BF16)


def three(ah, al, bh, bl, dims):
    (left,), (right,) = dims[0]
    return lax.dot_general(
        jnp.concatenate([ah, ah, al], axis=left),
        jnp.concatenate([bh, bl, bh], axis=right),
        dims,
        preferred_element_type=F32,
    )


def dot3(a, b, dims):
    return three(*split(a), *split(b), dims)


def tile_at(tile, index):
    return pl.ds(pl.multiple_of(index * tile, tile), tile)


def leading_kernel(
    tile,
    panels,
    places,
    where_ref,
    a_ref,
    high_ref,
    low_ref,
    top_ref,
    l_ref,
    lh_ref,
    ll_ref,
    s_ref,
    d_ref,
    acc_ref,
):
    rows = lax.broadcasted_iota(jnp.int32, (tile, tile), 0)
    cols = lax.broadcasted_iota(jnp.int32, (tile, tile), 1)
    diag = rows == cols
    eye = jnp.where(diag, 1.0, 0.0).astype(F32)
    weight = jnp.where(rows > cols, 1.0, jnp.where(diag, 0.5, 0.0)).astype(F32)

    at = functools.partial(tile_at, tile)
    for (i, j), (down, across) in places.items():
        s_ref[i * tile : (i + 1) * tile, j * tile : (j + 1) * tile] = a_ref[
            down * tile : (down + 1) * tile, across * tile : (across + 1) * tile
        ]
    l_ref[...] = jnp.zeros_like(l_ref)

    @pl.loop(0, panels)
    def _(k):
        here = at(k)
        block = s_ref[here, here]
        only = jnp.where(diag, block, 0.0)
        down = lax.rsqrt(jnp.sum(only, axis=1, keepdims=True))
        across = lax.rsqrt(jnp.sum(only, axis=0, keepdims=True))
        first = block * down * across - eye

        d_ref[here, :] = (eye - first * weight) * across

        def unfinished(state):
            step, worst = state
            return (worst > 1e-5) & (step < 16)

        def refine(state):
            step, _ = state
            w = d_ref[here, :]
            left = dot(dot(w, s_ref[here, here], NN), w, NT) - eye
            d_ref[here, :] = w - dot3(left * weight, w, NN)
            return step + 1, jnp.max(jnp.abs(left))

        lax.while_loop(unfinished, refine, (jnp.int32(0), jnp.float32(1.0)))
        dh, dl = split(d_ref[here, :])
        lower = three(*split(s_ref[here, here]), dh, dl, NT)
        l_ref[here, here] = jnp.where(rows >= cols, lower, 0.0)

        @pl.loop(k + 1, panels)
        def _(i):
            below = three(*split(s_ref[at(i), here]), *split(d_ref[here, :]), NT)
            l_ref[at(i), here] = below
            lh_ref[at(i), here], ll_ref[at(i), here] = split(below)

        @pl.loop(k + 1, panels)
        def _(i):
            @pl.loop(k + 1, i + 1)
            def _(j):
                s_ref[at(i), at(j)] -= three(
                    lh_ref[at(i), here],
                    ll_ref[at(i), here],
                    lh_ref[at(j), here],
                    ll_ref[at(j), here],
                    NT,
                )

    high_ref[...] = jnp.zeros_like(high_ref)
    low_ref[...] = jnp.zeros_like(low_ref)

    @pl.loop(0, panels)
    def _(i):
        high_ref[at(i), at(i)], low_ref[at(i), at(i)] = split(d_ref[at(i), :])

    @pl.loop(1, panels)
    def _(i):
        @pl.loop(0, i)
        def _(j):
            acc_ref[...] = jnp.zeros_like(acc_ref)

            @pl.loop(j, i)
            def _(m):
                acc_ref[...] += three(
                    lh_ref[at(i), at(m)],
                    ll_ref[at(i), at(m)],
                    high_ref[at(m), at(j)],
                    low_ref[at(m), at(j)],
                    NN,
                )

            entry = -three(
                high_ref[at(i), at(i)], low_ref[at(i), at(i)], *split(acc_ref[...]), NN
            )
            high_ref[at(i), at(j)], low_ref[at(i), at(j)] = split(entry)

    r = jnp.minimum(where_ref[0], panels - 1)
    c = jnp.minimum(where_ref[1], panels - 1)
    top_ref[...] = l_ref[at(r), at(c)]


def cut_kernel(child_ref, out_ref, wide_ref):
    pieces, deep, stored, tile = out_ref.shape
    lanes = wide_ref.shape[-1]
    for h in range(tile // lanes):
        across = slice(h * lanes, (h + 1) * lanes)
        wide_ref[h] = child_ref[:, :, across].astype(F32).reshape(wide_ref.shape[1:])
        for d in range(pieces):
            for e in range(deep):
                rows = wide_ref[h, pl.ds(d * deep + e, stored, stride=pieces * deep), :]
                out_ref[d, e, :, across] = rows.astype(BF16)


def cut_rows(child, devices):
    stored, tile, _ = child.shape
    deep = tile // devices
    block = 16
    return pl.pallas_call(
        cut_kernel,
        out_shape=jax.ShapeDtypeStruct((devices, deep, stored, tile), BF16),
        grid=(devices // block,),
        in_specs=[pl.BlockSpec((stored, block * deep, tile), lambda g: (0, g, 0))],
        out_specs=pl.BlockSpec((block, deep, stored, tile), lambda g: (g, 0, 0, 0)),
        scratch_shapes=[pltpu.VMEM((tile // 128, stored * block * deep, 128), F32)],
        compiler_params=pltpu.CompilerParams(vmem_limit_bytes=58 << 20),
        cost_estimate=pl.CostEstimate(
            flops=child.size, bytes_accessed=4 * child.size, transcendentals=0
        ),
        name="cut_rows",
    )(child)


def child_sum_kernel(target_ref, child_ref, out_ref):
    @pl.when(pl.program_id(0) == 0)
    def _():
        out_ref[...] = jnp.zeros_like(out_ref)

    sources, pieces, stored, tile = child_ref.shape
    count = sources * stored
    ids = lax.broadcasted_iota(jnp.int32, (out_ref.shape[0], count), 0)
    hot = jnp.where(ids == target_ref[0], 1.0, 0.0).astype(BF16)
    for e in range(pieces):
        right = child_ref[:, e].reshape(count, tile)
        out_ref[:, e * tile : (e + 1) * tile] += jnp.dot(hot, right, preferred_element_type=F32)


def child_sum(target, child, tiles):
    devices, pieces, stored, tile = child.shape
    block = 512 // stored
    return pl.pallas_call(
        child_sum_kernel,
        out_shape=jax.ShapeDtypeStruct((tiles, pieces * tile), F32),
        grid=(devices // block,),
        in_specs=[
            pl.BlockSpec((1, 1, block * stored), lambda g: (g, 0, 0)),
            pl.BlockSpec((block, pieces, stored, tile), lambda g: (g, 0, 0, 0)),
        ],
        out_specs=pl.BlockSpec((tiles, pieces * tile), lambda g: (0, 0)),
        compiler_params=pltpu.CompilerParams(vmem_limit_bytes=24 << 20),
        cost_estimate=pl.CostEstimate(
            flops=2 * tiles * child.size,
            bytes_accessed=2 * child.size + 4 * pieces * tiles * tile,
            transcendentals=0,
        ),
        name="child_sum",
    )(target.reshape(devices // block, 1, block * stored), child)


def whole_call(kernel, name, out_shape, args, scratch=(), scalars=0, limit=58, flops=0):
    whole = pl.BlockSpec(memory_space=pltpu.VMEM)
    moved = sum(x.size * x.dtype.itemsize for x in [*args, *out_shape])
    return pl.pallas_call(
        kernel,
        out_shape=out_shape,
        in_specs=[pl.BlockSpec(memory_space=pltpu.SMEM)] * scalars
        + [whole] * (len(args) - scalars),
        out_specs=[whole] * len(out_shape),
        scratch_shapes=scratch,
        compiler_params=pltpu.CompilerParams(vmem_limit_bytes=limit << 20),
        cost_estimate=pl.CostEstimate(flops=flops, bytes_accessed=moved, transcendentals=0),
        name=name,
    )(*args)


def encode_kernel(
    panels, rows, deep, sums_ref, base_ref, out_ref, x_ref, row_ref, col_ref
):
    devices, wide, tile = base_ref.shape
    cols = devices // rows
    slots = sums_ref.shape[0] // devices
    lrows = wide // deep
    lanes = 128
    each = tile // lanes
    groups = panels * each
    coded = groups * lanes
    lane = lax.broadcasted_iota(jnp.int32, (wide, lanes), 1)
    for r in range(rows):
        powers = [jnp.zeros((wide, lanes), F32)] * (deep + 1)
        for k in range(panels):
            first = (r * cols + k) * slots
            child = [
                sums_ref[first : first + lrows, e * tile : (e + 1) * tile] for e in range(deep)
            ]
            x = base_ref[r * cols + k] + jnp.concatenate(child, axis=0)
            top = jnp.maximum(jnp.max(jnp.abs(x), axis=1, keepdims=True), 1e-30)
            power = jnp.floor(jnp.log(top) * 1.4426950408889634) + 1.0
            code = jnp.round(x * jnp.exp2(15.0 - power))
            code = jnp.clip(code, -32767.0, 32767.0)
            powers = [jnp.where(lane == n * panels + k, power, p) for n, p in enumerate(powers)]
            for h in range(each):
                x_ref[k * each + h] = code[:, h * lanes : (h + 1) * lanes]
        for n in range(deep):
            power = powers[n][n * lrows : (n + 1) * lrows, :]
            row_power = power if n == 0 else row_power + power
        row_ref[r] = row_power
        x_ref[groups] = powers[deep]
        for u in range(cols // rows):
            col_ref[u * rows + r] = x_ref[groups, pl.ds(u, lrows, stride=wide // lrows), :]
        for g in range(groups):
            across = [slice(n * coded + g * lanes, n * coded + (g + 1) * lanes) for n in range(deep + 1)]
            for e in range(deep):
                piece = x_ref[g, e * lrows : (e + 1) * lrows, :]
                piece = piece.astype(jnp.int32).astype(jnp.int16)
                for c in range(cols):
                    out_ref[r * cols + c, :, across[e]] = piece
            for u in range(cols // rows):
                some = x_ref[g, pl.ds(u, lrows, stride=wide // lrows), :]
                some = some.astype(jnp.int32).astype(jnp.int16)
                for m in range(rows):
                    out_ref[m * cols + u * rows + r, :, across[deep]] = some
    for m in range(rows):
        for c in range(cols):
            power = (row_ref[m] + col_ref[c]).astype(jnp.int32).astype(jnp.int16)
            out_ref[m * cols + c, :, (deep + 1) * coded :] = power


def spread_rows(raw_ref, part, panels, out_ref, source, step, count, target):
    groups = out_ref.shape[0]
    last = raw_ref.shape[0] - 1
    scale = jnp.exp2(raw_ref[last, pl.ds(source, count, stride=step), :] - 15.0)
    for g in range(groups):
        k = part[1] * panels + g // (groups // panels)
        x = raw_ref[part[0] * groups + g, pl.ds(source, count, stride=step), :] * scale[:, k : k + 1]
        out_ref[g, pl.ds(target, count, stride=2), :] = x


def widen(code_ref, first, raw_ref):
    lanes = 128
    last = raw_ref.shape[0] - 1
    for g in range(last + 1):
        start = code_ref.shape[2] - lanes if g == last else first + g * lanes
        across = slice(start, start + lanes)
        raw_ref[g] = code_ref[:, :, across].astype(jnp.int32).astype(F32).reshape(raw_ref.shape[1:])


def column_kernel(
    tile,
    panels,
    where_ref,
    code_ref,
    wh_ref,
    wl_ref,
    gh_ref,
    gl_ref,
    raw_ref,
    nat_ref,
    xh_ref,
    xl_ref,
    acc_ref,
):
    at = functools.partial(tile_at, tile)
    devices, pieces, wide = code_ref.shape
    lcols = xh_ref.shape[1] // tile
    each = tile // 128
    deep = pieces // lcols
    widen(code_ref, wide - raw_ref.shape[0] * 128, raw_ref)
    for e in range(deep):
        for j in range(lcols):
            source, target = e * lcols + j, j * tile + e
            spread_rows(raw_ref, (0, deep), panels, nat_ref, source, pieces, devices, target)
    for k in range(panels):
        x = jnp.concatenate([nat_ref[k * each + h] for h in range(each)], axis=1)
        xh_ref[k], xl_ref[k] = split(x)

    @pl.loop(0, panels)
    def _(step):
        k = panels - 1 - step
        acc_ref[...] = jnp.zeros_like(acc_ref)

        @pl.loop(0, k + 1)
        def _(j):
            acc_ref[...] += three(
                xh_ref[j], xl_ref[j], wh_ref[at(k), at(j)], wl_ref[at(k), at(j)], NT
            )

        xh_ref[k], xl_ref[k] = split(acc_ref[...])

    @pl.loop(0, panels)
    def _(j):
        acc_ref[...] = jnp.zeros_like(acc_ref)

        @pl.loop(j, panels)
        def _(k):
            acc_ref[...] += three(
                xh_ref[k], xl_ref[k], wh_ref[at(k), at(j)], wl_ref[at(k), at(j)], NN
            )

        gh_ref[:, at(j)], gl_ref[:, at(j)] = split(acc_ref[...])

    my_col = where_ref[1]

    @pl.when(my_col < panels)
    def _():
        own = at(jnp.minimum(my_col, panels - 1))
        gh_ref[:tile] = wh_ref[own, :]
        gl_ref[:tile] = wl_ref[own, :]


def final_kernel(
    tile,
    panels,
    where_ref,
    code_ref,
    gh_ref,
    gl_ref,
    top_ref,
    sums_ref,
    front_ref,
    out_ref,
    raw_ref,
    nat_ref,
    sum_ref,
    add_ref,
):
    lanes = 128
    each = tile // lanes
    devices, pieces, _ = code_ref.shape
    lrows = front_ref.shape[0] // tile
    lcols = front_ref.shape[1] // tile
    groups = nat_ref.shape[0]
    deep = sums_ref.shape[2] // tile
    my_row = where_ref[0]
    my_col = where_ref[1]
    row_count = where_ref[2]
    factored = my_col < panels
    widen(code_ref, 0, raw_ref)
    for g in range(deep * each):
        sum_ref[g] = sums_ref[:, :, g * lanes : (g + 1) * lanes].reshape(sum_ref.shape[1:])

    @pl.loop(0, lrows)
    def _(i):
        rows = tile_at(tile, i)
        for e in range(deep):
            spread_rows(raw_ref, (e, e), panels, nat_ref, i, pieces, devices, e)
            for j in range(lcols):
                for h in range(each):
                    add_ref[j * each + h, pl.ds(e, devices, stride=2), :] = sum_ref[
                        e * each + h, pl.ds(j * lrows + i, devices, stride=lcols * lrows), :
                    ]
        x = jnp.concatenate([nat_ref[g] for g in range(nat_ref.shape[0])], axis=1)
        ah, al = split(x)
        leading = my_row + row_count * i < panels
        for j in range(lcols):
            here = slice(j * tile, (j + 1) * tile)
            product = three(ah, al, gh_ref[here], gl_ref[here], NT)
            child = jnp.concatenate([add_ref[j * each + h] for h in range(each)], axis=1)
            value = front_ref[rows, here] + child - product
            cleared = jnp.zeros_like(value)
            if j == 0:
                value = jnp.where(factored, product, value)
                cleared = jnp.where(factored, top_ref[...], cleared)
            value = jnp.where(leading, cleared, value)
            for h in range(each):
                start = i * (tile * lcols * each) + j * each + h
                out_ref[pl.ds(start, tile, stride=lcols * each), :] = value[
                    :, h * lanes : (h + 1) * lanes
                ]


def shards(parent_front, child_tiles, tile_target):
    lrows = parent_front.shape[0]
    tile = parent_front.shape[2]
    lcols = parent_front.shape[3]
    row_count = lax.axis_size("row")
    col_count = lax.axis_size("col")
    devices = row_count * col_count
    order = PANELS * tile
    half = order // 2
    part = tile // col_count
    deep = tile // devices
    slots = lrows * lcols
    lanes = 128
    groups = order // lanes
    my_row = lax.axis_index("row")
    my_col = lax.axis_index("col")
    where = jnp.stack([my_row, my_col, jnp.int32(row_count)]).astype(jnp.int32)
    stored = child_tiles.shape[1]
    shape = jax.ShapeDtypeStruct

    held = child_tiles.reshape(stored, tile, tile)
    cut = cut_rows(held, devices)

    mine = parent_front[0, 0, :, 0, 0, :].reshape(col_count, part, tile)
    mine = lax.all_to_all(mine, "col", 0, 0, tiled=True)
    mine, cut = lax.optimization_barrier((mine, cut))
    mine = mine[:PANELS].transpose(1, 0, 2).reshape(part, order)
    moved = lax.ppermute(mine[:, half:], "row", [(5, 6), (4, 7), (3, 0)])
    first = jnp.concatenate([mine[:, :tile], moved[:, : half - tile]], axis=1)
    packed = jnp.where(my_row >= PANELS, moved, jnp.where(my_row == 0, first, mine[:, :half]))
    places = {(i, j): (i, j) for i in range(PANELS) for j in range(min(i, 2) + 1)}
    places |= {(3, 3): (0, 1), (4, 3): (7, 0), (4, 4): (7, 1)}
    places |= {(5, 3): (6, 0), (5, 4): (6, 1), (5, 5): (6, 2)}
    cut, packed = lax.optimization_barrier((cut, packed))
    packed = lax.all_gather(packed, BOTH, axis=0, tiled=True)
    spread = lax.all_to_all(cut, BOTH, split_axis=0, concat_axis=0, tiled=True)
    later, _ = lax.optimization_barrier((parent_front, cut))
    base = later[:, 0, :, 0, 0, :].reshape(lrows, devices, deep, tile).transpose(1, 2, 0, 3)
    base = base.reshape(devices, deep * lrows, tile)
    front = later.reshape(lrows * tile, lcols * tile)
    spread, base, front = lax.optimization_barrier((spread, base, front))

    rows_all = tile_target[:, :, 0].reshape(-1)
    cols_all = tile_target[:, :, 1].reshape(-1)
    owner = rows_all % row_count * col_count + cols_all % col_count
    target = owner * slots + cols_all // col_count * lrows + rows_all // row_count
    base = lax.all_to_all(base, BOTH, split_axis=0, concat_axis=0, tiled=True)
    sums = child_sum(target, spread, devices * slots)

    (to_both,) = whole_call(
        functools.partial(encode_kernel, PANELS, row_count, deep),
        "encode",
        [shape((devices, lrows, (deep + 1) * order + lanes), jnp.int16)],
        [sums, base],
        scratch=[
            pltpu.VMEM((groups + 1, deep * lrows, lanes), F32),
            pltpu.VMEM((row_count, lrows, lanes), F32),
            pltpu.VMEM((col_count, lrows, lanes), F32),
        ],
        limit=32,
    )
    to_owner = sums.reshape(devices, slots, deep * tile).astype(F16)
    packed, _ = lax.optimization_barrier((packed, to_both))
    both = lax.all_to_all(to_both, BOTH, split_axis=0, concat_axis=0, tiled=True)
    *inverse, top = whole_call(
        functools.partial(leading_kernel, tile, PANELS, places),
        "leading",
        [shape((order, order), BF16)] * 2
        + [shape((tile, tile), F32)],
        [where, packed],
        scratch=[
            pltpu.VMEM((order, order), F32),
            pltpu.VMEM((order, order), BF16),
            pltpu.VMEM((order, order), BF16),
            pltpu.VMEM((order, order), F32),
            pltpu.VMEM((order, tile), F32),
            pltpu.VMEM((tile, tile), F32),
        ],
        scalars=1,
        limit=58,
        flops=24 * order**3,
    )
    to_owner, both, top = lax.optimization_barrier((to_owner, both, top))
    summed = lax.all_to_all(to_owner, BOTH, split_axis=0, concat_axis=0, tiled=True)

    right = whole_call(
        functools.partial(column_kernel, tile, PANELS),
        "column",
        [shape((lcols * tile, order), BF16)] * 2,
        [where, both, *inverse],
        scalars=1,
        scratch=[
            pltpu.VMEM((groups + 1, lcols * tile, lanes), F32),
            pltpu.VMEM((groups, lcols * tile, lanes), F32),
            pltpu.VMEM((PANELS, lcols * tile, tile), BF16),
            pltpu.VMEM((PANELS, lcols * tile, tile), BF16),
            pltpu.VMEM((lcols * tile, tile), F32),
        ],
        limit=58,
        flops=12 * lcols * tile * order**2,
    )
    (result,) = whole_call(
        functools.partial(final_kernel, tile, PANELS),
        "final",
        [shape((front.size // lanes, lanes), F32)],
        [where, both, *right, top, summed.astype(F32), front],
        scratch=[
            pltpu.VMEM((deep * groups + 1, devices * lrows, lanes), F32),
            pltpu.VMEM((groups, tile, lanes), F32),
            pltpu.VMEM((deep * tile // lanes, devices * slots, lanes), F32),
            pltpu.VMEM((lcols * tile // lanes, tile, lanes), F32),
        ],
        scalars=1,
        limit=58,
        flops=6 * lrows * tile * lcols * tile * order,
    )
    return result.reshape(parent_front.shape)


def solution(mesh):
    return jax.shard_map(
        shards,
        mesh=mesh,
        in_specs=(
            P(None, "row", None, None, "col", None),
            P(("row", "col"), None, None, None),
            P(),
        ),
        out_specs=P(None, "row", None, None, "col", None),
        check_vma=False,
    )
```

```python
import functools

import jax
import jax.numpy as jnp
from jax import lax
from jax.experimental import pallas as pl
from jax.experimental.pallas import tpu as pltpu
from jax.sharding import PartitionSpec as P

PANELS = 6
BOTH = ("row", "col")
F32 = jnp.float32
BF16 = jnp.bfloat16
F16 = jnp.float16
HIGHEST = lax.Precision.HIGHEST


NT = (((1,), (1,)), ((), ()))
NN = (((1,), (0,)), ((), ()))


def dot(a, b, dims, precision=HIGHEST):
    return lax.dot_general(a, b, dims, precision=precision, preferred_element_type=F32)


def split(x):
    high = x.astype(BF16)
    return high, (x - high.astype(F32)).astype(BF16)


def three(ah, al, bh, bl, dims):
    (left,), (right,) = dims[0]
    return lax.dot_general(
        jnp.concatenate([ah, ah, al], axis=left),
        jnp.concatenate([bh, bl, bh], axis=right),
        dims,
        preferred_element_type=F32,
    )


def dot3(a, b, dims):
    return three(*split(a), *split(b), dims)


def tile_at(tile, index):
    return pl.ds(pl.multiple_of(index * tile, tile), tile)


def leading_kernel(
    tile,
    panels,
    places,
    where_ref,
    a_ref,
    high_ref,
    low_ref,
    top_ref,
    l_ref,
    lh_ref,
    ll_ref,
    s_ref,
    d_ref,
    acc_ref,
):
    rows = lax.broadcasted_iota(jnp.int32, (tile, tile), 0)
    cols = lax.broadcasted_iota(jnp.int32, (tile, tile), 1)
    diag = rows == cols
    eye = jnp.where(diag, 1.0, 0.0).astype(F32)
    weight = jnp.where(rows > cols, 1.0, jnp.where(diag, 0.5, 0.0)).astype(F32)

    at = functools.partial(tile_at, tile)
    for (i, j), (down, across) in places.items():
        s_ref[i * tile : (i + 1) * tile, j * tile : (j + 1) * tile] = a_ref[
            down * tile : (down + 1) * tile, across * tile : (across + 1) * tile
        ]
    l_ref[...] = jnp.zeros_like(l_ref)

    @pl.loop(0, panels)
    def _(k):
        here = at(k)
        block = s_ref[here, here]
        only = jnp.where(diag, block, 0.0)
        down = lax.rsqrt(jnp.sum(only, axis=1, keepdims=True))
        across = lax.rsqrt(jnp.sum(only, axis=0, keepdims=True))
        first = block * down * across - eye

        d_ref[here, :] = (eye - first * weight) * across

        def unfinished(state):
            step, worst = state
            return (worst > 1e-5) & (step < 16)

        def refine(state):
            step, _ = state
            w = d_ref[here, :]
            left = dot(dot(w, s_ref[here, here], NN), w, NT) - eye
            d_ref[here, :] = w - dot3(left * weight, w, NN)
            return step + 1, jnp.max(jnp.abs(left))

        lax.while_loop(unfinished, refine, (jnp.int32(0), jnp.float32(1.0)))
        dh, dl = split(d_ref[here, :])
        lower = three(*split(s_ref[here, here]), dh, dl, NT)
        l_ref[here, here] = jnp.where(rows >= cols, lower, 0.0)

        @pl.loop(k + 1, panels)
        def _(i):
            below = three(*split(s_ref[at(i), here]), *split(d_ref[here, :]), NT)
            l_ref[at(i), here] = below
            lh_ref[at(i), here], ll_ref[at(i), here] = split(below)

        @pl.loop(k + 1, panels)
        def _(i):
            @pl.loop(k + 1, i + 1)
            def _(j):
                s_ref[at(i), at(j)] -= three(
                    lh_ref[at(i), here],
                    ll_ref[at(i), here],
                    lh_ref[at(j), here],
                    ll_ref[at(j), here],
                    NT,
                )

    high_ref[...] = jnp.zeros_like(high_ref)
    low_ref[...] = jnp.zeros_like(low_ref)

    @pl.loop(0, panels)
    def _(i):
        high_ref[at(i), at(i)], low_ref[at(i), at(i)] = split(d_ref[at(i), :])

    @pl.loop(1, panels)
    def _(i):
        @pl.loop(0, i)
        def _(j):
            acc_ref[...] = jnp.zeros_like(acc_ref)

            @pl.loop(j, i)
            def _(m):
                acc_ref[...] += three(
                    lh_ref[at(i), at(m)],
                    ll_ref[at(i), at(m)],
                    high_ref[at(m), at(j)],
                    low_ref[at(m), at(j)],
                    NN,
                )

            entry = -three(
                high_ref[at(i), at(i)], low_ref[at(i), at(i)], *split(acc_ref[...]), NN
            )
            high_ref[at(i), at(j)], low_ref[at(i), at(j)] = split(entry)

    r = jnp.minimum(where_ref[0], panels - 1)
    c = jnp.minimum(where_ref[1], panels - 1)
    top_ref[...] = l_ref[at(r), at(c)]


def cut_kernel(child_ref, out_ref, wide_ref):
    pieces, deep, stored, tile = out_ref.shape
    lanes = wide_ref.shape[-1]
    for h in range(tile // lanes):
        across = slice(h * lanes, (h + 1) * lanes)
        wide_ref[h] = child_ref[:, :, across].astype(F32).reshape(wide_ref.shape[1:])
        for d in range(pieces):
            for e in range(deep):
                rows = wide_ref[h, pl.ds(d * deep + e, stored, stride=pieces * deep), :]
                out_ref[d, e, :, across] = rows.astype(BF16)


def cut_rows(child, devices):
    stored, tile, _ = child.shape
    deep = tile // devices
    block = 16
    return pl.pallas_call(
        cut_kernel,
        out_shape=jax.ShapeDtypeStruct((devices, deep, stored, tile), BF16),
        grid=(devices // block,),
        in_specs=[pl.BlockSpec((stored, block * deep, tile), lambda g: (0, g, 0))],
        out_specs=pl.BlockSpec((block, deep, stored, tile), lambda g: (g, 0, 0, 0)),
        scratch_shapes=[pltpu.VMEM((tile // 128, stored * block * deep, 128), F32)],
        compiler_params=pltpu.CompilerParams(vmem_limit_bytes=58 << 20),
        cost_estimate=pl.CostEstimate(
            flops=child.size, bytes_accessed=4 * child.size, transcendentals=0
        ),
        name="cut_rows",
    )(child)


def child_sum_kernel(target_ref, child_ref, out_ref):
    @pl.when(pl.program_id(0) == 0)
    def _():
        out_ref[...] = jnp.zeros_like(out_ref)

    sources, pieces, stored, tile = child_ref.shape
    count = sources * stored
    ids = lax.broadcasted_iota(jnp.int32, (out_ref.shape[0], count), 0)
    hot = jnp.where(ids == target_ref[0], 1.0, 0.0).astype(BF16)
    for e in range(pieces):
        right = child_ref[:, e].reshape(count, tile)
        out_ref[:, e * tile : (e + 1) * tile] += jnp.dot(hot, right, preferred_element_type=F32)


def child_sum(target, child, tiles):
    devices, pieces, stored, tile = child.shape
    block = 512 // stored
    return pl.pallas_call(
        child_sum_kernel,
        out_shape=jax.ShapeDtypeStruct((tiles, pieces * tile), F32),
        grid=(devices // block,),
        in_specs=[
            pl.BlockSpec((1, 1, block * stored), lambda g: (g, 0, 0)),
            pl.BlockSpec((block, pieces, stored, tile), lambda g: (g, 0, 0, 0)),
        ],
        out_specs=pl.BlockSpec((tiles, pieces * tile), lambda g: (0, 0)),
        compiler_params=pltpu.CompilerParams(vmem_limit_bytes=24 << 20),
        cost_estimate=pl.CostEstimate(
            flops=2 * tiles * child.size,
            bytes_accessed=2 * child.size + 4 * pieces * tiles * tile,
            transcendentals=0,
        ),
        name="child_sum",
    )(target.reshape(devices // block, 1, block * stored), child)


def whole_call(kernel, name, out_shape, args, scratch=(), scalars=0, limit=58, flops=0):
    whole = pl.BlockSpec(memory_space=pltpu.VMEM)
    moved = sum(x.size * x.dtype.itemsize for x in [*args, *out_shape])
    return pl.pallas_call(
        kernel,
        out_shape=out_shape,
        in_specs=[pl.BlockSpec(memory_space=pltpu.SMEM)] * scalars
        + [whole] * (len(args) - scalars),
        out_specs=[whole] * len(out_shape),
        scratch_shapes=scratch,
        compiler_params=pltpu.CompilerParams(vmem_limit_bytes=limit << 20),
        cost_estimate=pl.CostEstimate(flops=flops, bytes_accessed=moved, transcendentals=0),
        name=name,
    )(*args)


def encode_kernel(
    panels, rows, deep, sums_ref, base_ref, out_ref, x_ref, row_ref, col_ref
):
    devices, wide, tile = base_ref.shape
    cols = devices // rows
    slots = sums_ref.shape[0] // devices
    lrows = wide // deep
    lanes = 128
    each = tile // lanes
    groups = panels * each
    coded = groups * lanes
    lane = lax.broadcasted_iota(jnp.int32, (wide, lanes), 1)
    for r in range(rows):
        powers = [jnp.zeros((wide, lanes), F32)] * (deep + 1)
        for k in range(panels):
            first = (r * cols + k) * slots
            child = [
                sums_ref[first : first + lrows, e * tile : (e + 1) * tile] for e in range(deep)
            ]
            x = base_ref[r * cols + k] + jnp.concatenate(child, axis=0)
            top = jnp.maximum(jnp.max(jnp.abs(x), axis=1, keepdims=True), 1e-30)
            power = jnp.floor(jnp.log(top) * 1.4426950408889634) + 1.0
            code = jnp.round(x * jnp.exp2(15.0 - power))
            code = jnp.clip(code, -32767.0, 32767.0)
            powers = [jnp.where(lane == n * panels + k, power, p) for n, p in enumerate(powers)]
            for h in range(each):
                x_ref[k * each + h] = code[:, h * lanes : (h + 1) * lanes]
        for n in range(deep):
            power = powers[n][n * lrows : (n + 1) * lrows, :]
            row_power = power if n == 0 else row_power + power
        row_ref[r] = row_power
        x_ref[groups] = powers[deep]
        for u in range(cols // rows):
            col_ref[u * rows + r] = x_ref[groups, pl.ds(u, lrows, stride=wide // lrows), :]
        for g in range(groups):
            across = [slice(n * coded + g * lanes, n * coded + (g + 1) * lanes) for n in range(deep + 1)]
            for e in range(deep):
                piece = x_ref[g, e * lrows : (e + 1) * lrows, :]
                piece = piece.astype(jnp.int32).astype(jnp.int16)
                for c in range(cols):
                    out_ref[r * cols + c, :, across[e]] = piece
            for u in range(cols // rows):
                some = x_ref[g, pl.ds(u, lrows, stride=wide // lrows), :]
                some = some.astype(jnp.int32).astype(jnp.int16)
                for m in range(rows):
                    out_ref[m * cols + u * rows + r, :, across[deep]] = some
    for m in range(rows):
        for c in range(cols):
            power = (row_ref[m] + col_ref[c]).astype(jnp.int32).astype(jnp.int16)
            out_ref[m * cols + c, :, (deep + 1) * coded :] = power


def spread_rows(raw_ref, part, panels, out_ref, source, step, count, target):
    groups = out_ref.shape[0]
    last = raw_ref.shape[0] - 1
    scale = jnp.exp2(raw_ref[last, pl.ds(source, count, stride=step), :] - 15.0)
    for g in range(groups):
        k = part[1] * panels + g // (groups // panels)
        x = raw_ref[part[0] * groups + g, pl.ds(source, count, stride=step), :] * scale[:, k : k + 1]
        out_ref[g, pl.ds(target, count, stride=2), :] = x


def widen(code_ref, first, raw_ref):
    lanes = 128
    last = raw_ref.shape[0] - 1
    for g in range(last + 1):
        start = code_ref.shape[2] - lanes if g == last else first + g * lanes
        across = slice(start, start + lanes)
        raw_ref[g] = code_ref[:, :, across].astype(jnp.int32).astype(F32).reshape(raw_ref.shape[1:])


def column_kernel(
    tile,
    panels,
    where_ref,
    code_ref,
    wh_ref,
    wl_ref,
    gh_ref,
    gl_ref,
    raw_ref,
    nat_ref,
    xh_ref,
    xl_ref,
    acc_ref,
):
    at = functools.partial(tile_at, tile)
    devices, pieces, wide = code_ref.shape
    lcols = xh_ref.shape[1] // tile
    each = tile // 128
    deep = pieces // lcols
    widen(code_ref, wide - raw_ref.shape[0] * 128, raw_ref)
    for e in range(deep):
        for j in range(lcols):
            source, target = e * lcols + j, j * tile + e
            spread_rows(raw_ref, (0, deep), panels, nat_ref, source, pieces, devices, target)
    for k in range(panels):
        x = jnp.concatenate([nat_ref[k * each + h] for h in range(each)], axis=1)
        xh_ref[k], xl_ref[k] = split(x)

    @pl.loop(0, panels)
    def _(step):
        k = panels - 1 - step
        acc_ref[...] = jnp.zeros_like(acc_ref)

        @pl.loop(0, k + 1)
        def _(j):
            acc_ref[...] += three(
                xh_ref[j], xl_ref[j], wh_ref[at(k), at(j)], wl_ref[at(k), at(j)], NT
            )

        xh_ref[k], xl_ref[k] = split(acc_ref[...])

    @pl.loop(0, panels)
    def _(j):
        acc_ref[...] = jnp.zeros_like(acc_ref)

        @pl.loop(j, panels)
        def _(k):
            acc_ref[...] += three(
                xh_ref[k], xl_ref[k], wh_ref[at(k), at(j)], wl_ref[at(k), at(j)], NN
            )

        gh_ref[:, at(j)], gl_ref[:, at(j)] = split(acc_ref[...])

    my_col = where_ref[1]

    @pl.when(my_col < panels)
    def _():
        own = at(jnp.minimum(my_col, panels - 1))
        gh_ref[:tile] = wh_ref[own, :]
        gl_ref[:tile] = wl_ref[own, :]


def final_kernel(
    tile,
    panels,
    where_ref,
    code_ref,
    gh_ref,
    gl_ref,
    top_ref,
    sums_ref,
    front_ref,
    out_ref,
    raw_ref,
    nat_ref,
    sum_ref,
    add_ref,
):
    lanes = 128
    each = tile // lanes
    devices, pieces, _ = code_ref.shape
    lrows = front_ref.shape[0] // tile
    lcols = front_ref.shape[1] // tile
    groups = nat_ref.shape[0]
    deep = sums_ref.shape[2] // tile
    my_row = where_ref[0]
    my_col = where_ref[1]
    row_count = where_ref[2]
    factored = my_col < panels
    widen(code_ref, 0, raw_ref)
    for g in range(deep * each):
        sum_ref[g] = sums_ref[:, :, g * lanes : (g + 1) * lanes].reshape(sum_ref.shape[1:])

    @pl.loop(0, lrows)
    def _(i):
        rows = tile_at(tile, i)
        for e in range(deep):
            spread_rows(raw_ref, (e, e), panels, nat_ref, i, pieces, devices, e)
            for j in range(lcols):
                for h in range(each):
                    add_ref[j * each + h, pl.ds(e, devices, stride=2), :] = sum_ref[
                        e * each + h, pl.ds(j * lrows + i, devices, stride=lcols * lrows), :
                    ]
        x = jnp.concatenate([nat_ref[g] for g in range(nat_ref.shape[0])], axis=1)
        ah, al = split(x)
        leading = my_row + row_count * i < panels
        for j in range(lcols):
            here = slice(j * tile, (j + 1) * tile)
            product = three(ah, al, gh_ref[here], gl_ref[here], NT)
            child = jnp.concatenate([add_ref[j * each + h] for h in range(each)], axis=1)
            value = front_ref[rows, here] + child - product
            cleared = jnp.zeros_like(value)
            if j == 0:
                value = jnp.where(factored, product, value)
                cleared = jnp.where(factored, top_ref[...], cleared)
            value = jnp.where(leading, cleared, value)
            for h in range(each):
                start = i * (tile * lcols * each) + j * each + h
                out_ref[pl.ds(start, tile, stride=lcols * each), :] = value[
                    :, h * lanes : (h + 1) * lanes
                ]


def shards(parent_front, child_tiles, tile_target):
    lrows = parent_front.shape[0]
    tile = parent_front.shape[2]
    lcols = parent_front.shape[3]
    row_count = lax.axis_size("row")
    col_count = lax.axis_size("col")
    devices = row_count * col_count
    order = PANELS * tile
    half = order // 2
    part = tile // col_count
    deep = tile // devices
    slots = lrows * lcols
    lanes = 128
    groups = order // lanes
    my_row = lax.axis_index("row")
    my_col = lax.axis_index("col")
    where = jnp.stack([my_row, my_col, jnp.int32(row_count)]).astype(jnp.int32)
    stored = child_tiles.shape[1]
    shape = jax.ShapeDtypeStruct

    held = child_tiles.reshape(stored, tile, tile)
    cut = cut_rows(held, devices)

    mine = parent_front[0, 0, :, 0, 0, :].reshape(col_count, part, tile)
    mine = lax.all_to_all(mine, "col", 0, 0, tiled=True)
    mine, cut = lax.optimization_barrier((mine, cut))
    mine = mine[:PANELS].transpose(1, 0, 2).reshape(part, order)
    moved = lax.ppermute(mine[:, half:], "row", [(5, 6), (4, 7), (3, 0)])
    first = jnp.concatenate([mine[:, :tile], moved[:, : half - tile]], axis=1)
    packed = jnp.where(my_row >= PANELS, moved, jnp.where(my_row == 0, first, mine[:, :half]))
    places = {(i, j): (i, j) for i in range(PANELS) for j in range(min(i, 2) + 1)}
    places |= {(3, 3): (0, 1), (4, 3): (7, 0), (4, 4): (7, 1)}
    places |= {(5, 3): (6, 0), (5, 4): (6, 1), (5, 5): (6, 2)}
    packed = lax.all_gather(packed, BOTH, axis=0, tiled=True)
    spread = lax.all_to_all(cut, BOTH, split_axis=0, concat_axis=0, tiled=True)
    later, _ = lax.optimization_barrier((parent_front, cut))
    base = later[:, 0, :, 0, 0, :].reshape(lrows, devices, deep, tile).transpose(1, 2, 0, 3)
    base = base.reshape(devices, deep * lrows, tile)
    front = later.reshape(lrows * tile, lcols * tile)
    spread, base, front = lax.optimization_barrier((spread, base, front))

    rows_all = tile_target[:, :, 0].reshape(-1)
    cols_all = tile_target[:, :, 1].reshape(-1)
    owner = rows_all % row_count * col_count + cols_all % col_count
    target = owner * slots + cols_all // col_count * lrows + rows_all // row_count
    base = lax.all_to_all(base, BOTH, split_axis=0, concat_axis=0, tiled=True)
    sums = child_sum(target, spread, devices * slots)

    (to_both,) = whole_call(
        functools.partial(encode_kernel, PANELS, row_count, deep),
        "encode",
        [shape((devices, lrows, (deep + 1) * order + lanes), jnp.int16)],
        [sums, base],
        scratch=[
            pltpu.VMEM((groups + 1, deep * lrows, lanes), F32),
            pltpu.VMEM((row_count, lrows, lanes), F32),
            pltpu.VMEM((col_count, lrows, lanes), F32),
        ],
        limit=32,
    )
    to_owner = sums.reshape(devices, slots, deep * tile).astype(F16)
    packed, _ = lax.optimization_barrier((packed, to_both))
    both = lax.all_to_all(to_both, BOTH, split_axis=0, concat_axis=0, tiled=True)
    *inverse, top = whole_call(
        functools.partial(leading_kernel, tile, PANELS, places),
        "leading",
        [shape((order, order), BF16)] * 2
        + [shape((tile, tile), F32)],
        [where, packed],
        scratch=[
            pltpu.VMEM((order, order), F32),
            pltpu.VMEM((order, order), BF16),
            pltpu.VMEM((order, order), BF16),
            pltpu.VMEM((order, order), F32),
            pltpu.VMEM((order, tile), F32),
            pltpu.VMEM((tile, tile), F32),
        ],
        scalars=1,
        limit=58,
        flops=24 * order**3,
    )
    to_owner, both, top = lax.optimization_barrier((to_owner, both, top))
    summed = lax.all_to_all(to_owner, BOTH, split_axis=0, concat_axis=0, tiled=True)

    right = whole_call(
        functools.partial(column_kernel, tile, PANELS),
        "column",
        [shape((lcols * tile, order), BF16)] * 2,
        [where, both, *inverse],
        scalars=1,
        scratch=[
            pltpu.VMEM((groups + 1, lcols * tile, lanes), F32),
            pltpu.VMEM((groups, lcols * tile, lanes), F32),
            pltpu.VMEM((PANELS, lcols * tile, tile), BF16),
            pltpu.VMEM((PANELS, lcols * tile, tile), BF16),
            pltpu.VMEM((lcols * tile, tile), F32),
        ],
        limit=58,
        flops=12 * lcols * tile * order**2,
    )
    (result,) = whole_call(
        functools.partial(final_kernel, tile, PANELS),
        "final",
        [shape((front.size // lanes, lanes), F32)],
        [where, both, *right, top, summed.astype(F32), front],
        scratch=[
            pltpu.VMEM((deep * groups + 1, devices * lrows, lanes), F32),
            pltpu.VMEM((groups, tile, lanes), F32),
            pltpu.VMEM((deep * tile // lanes, devices * slots, lanes), F32),
            pltpu.VMEM((lcols * tile // lanes, tile, lanes), F32),
        ],
        scalars=1,
        limit=58,
        flops=6 * lrows * tile * lcols * tile * order,
    )
    return result.reshape(parent_front.shape)


def solution(mesh):
    return jax.shard_map(
        shards,
        mesh=mesh,
        in_specs=(
            P(None, "row", None, None, "col", None),
            P(("row", "col"), None, None, None),
            P(),
        ),
        out_specs=P(None, "row", None, None, "col", None),
        check_vma=False,
    )
```
